512 devices in a mesh: energy: 32 (over z, core), slab: 16 (over y, x).
Axes of the slice: x: 4, y: 4, z: 16, core: 2. Of those that a mesh axis runs over, the one named last changes fastest.
Arguments:
- retarded: bfloat16 [16, 768, 2, 128, 128], P('slab', 'energy'), may hold values from -0.5 to 0.5
- self_lesser: bfloat16 [16, 768, 2, 128, 128], P('slab', 'energy'), may hold values from -6 to 6
- coupling: bfloat16 [4, 2, 128, 128], replicated, may hold values from -0.1875 to 0.1875
- occupancy: float32 [4], replicated, may hold values from 0.2 to 4
- adaptive_owner: int32 [384], replicated, may hold values from 0 to 31, as said below
- phonon_offsets: int32 [4], replicated, may hold values from 1 to 12, as said below
Outputs:
- phonon_lesser: float32 [16, 384, 2, 128, 128], P('slab', 'energy')
The draws below stay inside these ranges and needn't reach their ends.
Inputs may be any that keep to these rules, and one draw needn't show every extreme that they name: `adaptive_owner`: each energy device holds at least one and at most 24 energies, and one or more hold exactly 24. Of the 12 energies e that share e // 12, no device holds more than 1, and some device holds exactly 1 of some such block. `phonon_offsets`: one of the offsets equals 12 and another one equals 1.
All inputs are finite; a program needn't handle non-finite values.
Results may differ from the reference program's by a relative error of at most 0.0064.
Values may be sent and summed in bfloat16 or wider, within the bound.
A program may use at most 64 MiB of HBM per device.

```python
import math
import jax
import jax.numpy as jnp
from jax import lax

NB = 128
MODES = 4
E_DEV = 12
CAP = 24
ENERGIES = 384
SLABS = 16
N_ENERGY = 32


def draw_adaptive_owner(key, part):
    groups = ENERGIES // E_DEV
    half_count = E_DEV // 2
    heavy_count = groups // 4
    block_index = jnp.arange(groups, dtype=jnp.int32)[:, None]
    within = jnp.arange(E_DEV, dtype=jnp.int32)[None, :]
    heavy_order = within * groups + block_index
    heavy_owner = heavy_order // (2 * E_DEV)
    light_order = (within - half_count) * groups + block_index
    light_owner = heavy_count + light_order * (groups - heavy_count) // (groups * half_count)
    base_owner = jnp.where(within < half_count, heavy_owner, light_owner)
    shuffled = jax.random.permutation(jax.random.fold_in(key, 11), groups).astype(jnp.int32)
    owners = shuffled[base_owner]
    block_keys = jax.random.split(jax.random.fold_in(key, 12), groups)
    placing = jax.vmap(lambda sub_key: jax.random.permutation(sub_key, E_DEV))(block_keys).astype(jnp.int32)
    energy_slot = (block_index * E_DEV + placing).reshape(-1)
    return jnp.zeros((ENERGIES,), jnp.int32).at[energy_slot].set(owners.reshape(-1).astype(jnp.int32))


def draw_phonon_offsets(key, part):
    picked = jax.random.randint(jax.random.fold_in(key, 21), (MODES,), 1, E_DEV + 1)
    widest = jax.random.randint(jax.random.fold_in(key, 22), (), 0, MODES)
    narrowest = (widest + 1) % MODES
    modes = jnp.arange(MODES)
    offsets = jnp.where(modes == widest, E_DEV, picked)
    offsets = jnp.where(modes == narrowest, 1, offsets)
    return offsets.astype(jnp.int32)


def block_scale(own_key, dims, pieces, low, high):
    def one(position, blocks):
        draws = jax.random.uniform(jax.random.fold_in(jax.random.fold_in(own_key, 6), position), (blocks,), jnp.float32, low / len(pieces), high / len(pieces))
        return jnp.repeat(jnp.exp(draws), dims[position] // blocks).reshape((-1,) + (1,) * (len(dims) - position - 1))

    gain = one(*pieces[0])
    for cut in pieces[1:]:
        gain = gain * one(*cut)
    return gain


def normal_values(own_key, extent, deviation, most, shards=(), kind=jnp.bfloat16):
    loudness = block_scale(own_key, extent, shards, -0.22, 0.18) if shards else 1.0
    values = jax.random.normal(own_key, extent, jnp.float32) * deviation * loudness
    return jnp.minimum(jnp.maximum(values, -most), most).astype(kind)


def setup_inputs(seed: int = 0) -> dict:
    keys = jax.random.split(jax.random.key(seed), 7)
    retarded = normal_values(keys[0], (SLABS, N_ENERGY * CAP, 2, NB, NB), NB ** -0.5, 0.5, ((0, 16), (1, 32)))
    self_lesser = normal_values(keys[1], (SLABS, N_ENERGY * CAP, 2, NB, NB), 1.0, 6.0, ((0, 16), (1, 32)))
    coupling = normal_values(keys[2], (MODES, 2, NB, NB), (8 * NB) ** -0.5, 0.1875)
    occupancy = jnp.clip(jnp.exp(jax.random.uniform(keys[3], (MODES,), jnp.float32, math.log(0.2), math.log(4.0))), 0.2, 4.0)
    adaptive_owner = draw_adaptive_owner(jax.random.fold_in(keys[6], 71), 0)
    phonon_offsets = draw_phonon_offsets(jax.random.fold_in(keys[6], 71), 0)
    return {"retarded": retarded, "self_lesser": self_lesser, "coupling": coupling, "occupancy": occupancy, "adaptive_owner": adaptive_owner, "phonon_offsets": phonon_offsets}


def batched(left_block, right_block):
    return jnp.einsum("jab,jbc->jac", left_block.astype(jnp.float32), right_block.astype(jnp.float32))


def batched_transposed(left_block, right_block):
    return jnp.einsum("jab,jcb->jac", left_block.astype(jnp.float32), right_block.astype(jnp.float32))


def lesser_blocks(green_ret, sigma_total):
    ret_real, ret_imag = green_ret[:, 0], green_ret[:, 1]
    sig_real, sig_imag = sigma_total[:, 0], sigma_total[:, 1]
    half_real = batched(ret_real, sig_real) - batched(ret_imag, sig_imag)
    half_imag = batched(ret_real, sig_imag) + batched(ret_imag, sig_real)
    half_product = jnp.stack([half_real, half_imag], 1).astype(jnp.bfloat16)
    hp_real, hp_imag = half_product[:, 0], half_product[:, 1]
    out_real = batched_transposed(hp_real, ret_real) + batched_transposed(hp_imag, ret_imag)
    out_imag = batched_transposed(hp_imag, ret_real) - batched_transposed(hp_real, ret_imag)
    return jnp.stack([out_real, out_imag], 1).astype(jnp.bfloat16)


def sandwich(coupling_mode, weighted):
    m_real = coupling_mode[0].astype(jnp.float32)
    m_imag = coupling_mode[1].astype(jnp.float32)
    w_real = weighted[:, 0].astype(jnp.float32)
    w_imag = weighted[:, 1].astype(jnp.float32)
    left_real = jnp.einsum("ab,jbc->jac", m_real, w_real) - jnp.einsum("ab,jbc->jac", m_imag, w_imag)
    left_imag = jnp.einsum("ab,jbc->jac", m_real, w_imag) + jnp.einsum("ab,jbc->jac", m_imag, w_real)
    coupled = jnp.stack([left_real, left_imag], 1).astype(jnp.bfloat16).astype(jnp.float32)
    c_real, c_imag = coupled[:, 0], coupled[:, 1]
    out_real = jnp.einsum("jab,cb->jac", c_real, m_real) + jnp.einsum("jab,cb->jac", c_imag, m_imag)
    out_imag = jnp.einsum("jab,cb->jac", c_imag, m_real) - jnp.einsum("jab,cb->jac", c_real, m_imag)
    return jnp.stack([out_real, out_imag], 1)


def reference(retarded, self_lesser, coupling, occupancy, adaptive_owner, phonon_offsets):
    positions = jnp.arange(ENERGIES, dtype=jnp.int32)
    same_owner = adaptive_owner[:, None] == adaptive_owner[None, :]
    earlier = same_owner & (positions[None, :] < positions[:, None])
    slot_rank = jnp.sum(earlier.astype(jnp.int32), axis=1).astype(jnp.int32)
    entries = (adaptive_owner * CAP + slot_rank).astype(jnp.int32)

    def select_slab(source, slab_number):
        clamped = jnp.clip(slab_number, 0, SLABS - 1).astype(jnp.int32)
        whole_slab = lax.dynamic_index_in_dim(source, clamped, 0, keepdims=False)
        inside = ((slab_number >= 0) & (slab_number < SLABS)).astype(jnp.float32)
        return jnp.take(whole_slab, entries, axis=0).astype(jnp.float32) * inside

    def per_slab(slab_index):
        own_sigma = select_slab(self_lesser, slab_index)
        lower_sigma = select_slab(self_lesser, slab_index - 1)
        upper_sigma = select_slab(self_lesser, slab_index + 1)
        sigma_total = (own_sigma + 0.5 * (lower_sigma + upper_sigma)).astype(jnp.bfloat16)
        green_ret = jnp.take(lax.dynamic_index_in_dim(retarded, slab_index, 0, keepdims=False), entries, axis=0)
        lesser = lesser_blocks(green_ret, sigma_total)
        accumulated = jnp.zeros((ENERGIES, 2, NB, NB), jnp.float32)
        for phonon_mode in range(MODES):
            offset = phonon_offsets[phonon_mode]
            shifted_up = jnp.roll(lesser, -offset, axis=0).astype(jnp.float32)
            shifted_down = jnp.roll(lesser, offset, axis=0).astype(jnp.float32)
            weight_one = occupancy[phonon_mode]
            weighted = ((weight_one + 1.0) * shifted_up + weight_one * shifted_down).astype(jnp.bfloat16)
            accumulated = accumulated + sandwich(coupling[phonon_mode], weighted)
        return accumulated

    return lax.map(per_slab, jnp.arange(SLABS, dtype=jnp.int32))
```

```python
import functools

import jax
import jax.numpy as jnp
from jax import lax
from jax.experimental import pallas as pl
from jax.experimental.pallas import tpu as pltpu
from jax.sharding import PartitionSpec as P

MESH = pl.DeviceIdType.MESH
LAG = 5
START = 3
PLAG = 3
AHEAD = 6
STEPS = 112
SIZES = (88, 104)


def with_halo(array, sides, width, wrap):
    for axis, dim in sides:
        peers, length = (lax.axis_size(axis), array.shape[dim])
        up = [(i, (i + 1) % peers) for i in range(peers if wrap else peers - 1)]
        down = [(j, i) for i, j in up]
        last = lax.slice_in_dim(array, length - width, length, axis=dim)
        initial = lax.slice_in_dim(array, 0, width, axis=dim)
        before = lax.ppermute(last, axis, up)
        after = lax.ppermute(initial, axis, down)
        array = jnp.concatenate([before, array, after], axis=dim)
    return array


def batched(left_block, right_block):
    return jnp.einsum("jab,jbc->jac", left_block, right_block, preferred_element_type=jnp.float32)


def batched_transposed(left_block, right_block):
    return jnp.einsum("jab,jcb->jac", left_block, right_block, preferred_element_type=jnp.float32)


def lesser_blocks(green_ret, sigma_total):
    ret_real, ret_imag = (green_ret[:, 0], green_ret[:, 1])
    sig_real, sig_imag = (sigma_total[:, 0], sigma_total[:, 1])
    half_real = batched(ret_real, sig_real) - batched(ret_imag, sig_imag)
    half_imag = batched(ret_real, sig_imag) + batched(ret_imag, sig_real)
    half_product = jnp.stack([half_real, half_imag], 1).astype(jnp.bfloat16)
    hp_real, hp_imag = (half_product[:, 0], half_product[:, 1])
    out_real = batched_transposed(hp_real, ret_real) + batched_transposed(hp_imag, ret_imag)
    out_imag = batched_transposed(hp_imag, ret_real) - batched_transposed(hp_real, ret_imag)
    return jnp.stack([out_real, out_imag], 1).astype(jnp.bfloat16)


def combined(stacked_rims):
    own_sigma = stacked_rims[1].astype(jnp.float32)
    beside = stacked_rims[0].astype(jnp.float32) + stacked_rims[2].astype(jnp.float32)
    return (own_sigma + 0.5 * beside).astype(jnp.bfloat16)


def sandwich(coupling_mode, weighted):
    m_real, m_imag = (coupling_mode[0], coupling_mode[1])
    w_real, w_imag = (weighted[:, 0], weighted[:, 1])
    left_real = jnp.einsum(
        "ab,jbc->jac", m_real, w_real, preferred_element_type=jnp.float32
    ) - jnp.einsum("ab,jbc->jac", m_imag, w_imag, preferred_element_type=jnp.float32)
    left_imag = jnp.einsum(
        "ab,jbc->jac", m_real, w_imag, preferred_element_type=jnp.float32
    ) + jnp.einsum("ab,jbc->jac", m_imag, w_real, preferred_element_type=jnp.float32)
    coupled = jnp.stack([left_real, left_imag], 1).astype(jnp.bfloat16)
    c_real, c_imag = (coupled[:, 0], coupled[:, 1])
    out_real = jnp.einsum(
        "jab,cb->jac", c_real, m_real, preferred_element_type=jnp.float32
    ) + jnp.einsum("jab,cb->jac", c_imag, m_imag, preferred_element_type=jnp.float32)
    out_imag = jnp.einsum(
        "jab,cb->jac", c_imag, m_real, preferred_element_type=jnp.float32
    ) - jnp.einsum("jab,cb->jac", c_real, m_imag, preferred_element_type=jnp.float32)
    return jnp.stack([out_real, out_imag], 1)


def general(retarded, self_lesser, coupling, occupancy, adaptive_owner, phonon_offsets):
    n_energy = lax.axis_size("energy")
    my_index = lax.axis_index("energy")
    energies = adaptive_owner.shape[0]
    per_device = energies // n_energy
    capacity = retarded.shape[1]
    slot_count = -(-capacity // n_energy)
    positions = jnp.arange(energies, dtype=jnp.int32)
    block_of = positions // per_device
    same_owner = adaptive_owner[:, None] == adaptive_owner[None, :]
    earlier = same_owner & (positions[None, :] < positions[:, None])
    slot_rank = jnp.sum(earlier.astype(jnp.int32), axis=1)
    same_block = block_of[None, :] == block_of[:, None]
    group_rank = jnp.sum((earlier & same_block).astype(jnp.int32), axis=1)
    target = block_of * slot_count + group_rank
    targets = jnp.arange(n_energy * slot_count, dtype=jnp.int32)
    matches = (adaptive_owner == my_index)[None, :] & (target[None, :] == targets[:, None])
    send_slot = jnp.sum(jnp.where(matches, slot_rank[None, :], 0), axis=1)
    first_energy = my_index * per_device
    own_owner = lax.dynamic_slice_in_dim(adaptive_owner, first_energy, per_device)
    own_rank = lax.dynamic_slice_in_dim(group_rank, first_energy, per_device)
    receive_slot = own_owner * slot_count + own_rank
    stacked_rims = with_halo(self_lesser, (("slab", 0),), 1, False)
    formed = lesser_blocks(retarded[0], combined(stacked_rims))
    outgoing = jnp.take(formed, send_slot, axis=0)
    arrived = lax.all_to_all(outgoing, "energy", split_axis=0, concat_axis=0, tiled=True)
    lesser = jnp.take(arrived, receive_slot, axis=0)
    widened = with_halo(lesser, (("energy", 0),), per_device, True)
    accumulated = jnp.zeros((per_device, 2, lesser.shape[2], lesser.shape[3]), jnp.float32)
    for phonon_mode in range(coupling.shape[0]):
        offset = phonon_offsets[phonon_mode]
        shifted_up = lax.dynamic_slice_in_dim(widened, per_device + offset, per_device, 0).astype(
            jnp.float32
        )
        shifted_down = lax.dynamic_slice_in_dim(widened, per_device - offset, per_device, 0).astype(
            jnp.float32
        )
        weight_one = occupancy[phonon_mode]
        weighted = ((weight_one + 1.0) * shifted_up + weight_one * shifted_down).astype(
            jnp.bfloat16
        )
        accumulated = accumulated + sandwich(coupling[phonon_mode], weighted)
    return accumulated[None]


def packets(owner):
    e = jnp.arange(384, dtype=jnp.int32)
    chip, upper = owner // 2, (e // 12) % 2 == 1
    d = (e // 24 - chip + 16) % 16
    plus = jnp.where(upper, d <= 7, (d >= 1) & (d <= 8))
    there = jnp.where(upper, d + 1, d)
    back = jnp.where(upper, 16 - d, jnp.where(d == 0, 1, 17 - d))
    reach = jnp.where(plus, there, back)
    way = jnp.where(plus, 0, 1)
    stop = jnp.where(plus, chip, (16 - chip) % 16)
    train = way * 16 + stop
    key = (8 - reach) * 384 + e
    same = owner[:, None] == owner[None, :]
    before = key[None, :] < key[:, None]
    rank = jnp.sum((same & before).astype(jnp.int32), axis=1)
    slot = jnp.sum((same & (e[None, :] < e[:, None])).astype(jnp.int32), axis=1)
    place = jnp.sum(((train[:, None] == train[None, :]) & before).astype(jnp.int32), axis=1)
    return way, stop, train, reach, rank, slot, place


def counts(train, reach, rank, place):
    lane = jnp.arange(128, dtype=jnp.int32)
    hops = jnp.arange(8, dtype=jnp.int32)
    source = (lane // 16) * 16 + (lane[None, :] - hops[:, None] + 16) % 16
    through = (source[:, :, None] == train[None, None, :]) & (reach[None, None, :] > hops[:, None, None])
    passing = jnp.sum(through.astype(jnp.int32), axis=2)
    ready = jnp.arange(32, dtype=jnp.int32)
    held = (lane[None, :, None] == train[None, None, :]) & (rank[None, None, :] >= ready[:, None, None])
    first = jnp.min(jnp.where(held, place[None, None, :], 384), axis=2)
    return passing, jnp.minimum(first, passing[:1])


def schedule_kernel(passing_ref, ready_ref, code_ref, sent_ref):
    lane = lax.broadcasted_iota(jnp.int32, (1, 128), 1)
    edge = lane % 16 == 0
    limit = [passing_ref[i : i + 1, :] for i in range(8)]
    zero = jnp.zeros((1, 128), jnp.int32)
    for t in range(LAG):
        sent_ref[t] = jnp.zeros((8, 128), jnp.int32)

    def slot(t, sent):
        ready = jnp.clip((t - START + 2) // 2, 0, 24)
        code = zero - 1
        taken = lane < 0
        out = []
        for i in range(8):
            if i == 0:
                there = ready_ref[pl.ds(ready, 1), :]
            else:
                old = sent_ref[t, i - 1 : i, :]
                there = jnp.where(edge, pltpu.roll(old, 113, 1), pltpu.roll(old, 1, 1))
                there = jnp.minimum(there, limit[i])
            go = (sent[i] < there) & ~taken
            code = jnp.where(go, sent[i] + 64 * i, code)
            taken = taken | go
            out.append(jnp.where(go, sent[i] + 1, sent[i]))
            sent_ref[t + LAG, i : i + 1, :] = out[i]
        code_ref[pl.ds(t, 1), :] = code
        return tuple(out)

    lax.fori_loop(0, STEPS, slot, (zero,) * 8)


def schedule(passing, ready):
    return pl.pallas_call(
        schedule_kernel,
        out_shape=jax.ShapeDtypeStruct((STEPS, 128), jnp.int32),
        in_specs=[pl.BlockSpec(memory_space=pltpu.VMEM)] * 2,
        out_specs=pl.BlockSpec(memory_space=pltpu.VMEM),
        scratch_shapes=[pltpu.VMEM((STEPS + LAG, 8, 128), jnp.int32)],
    )(passing, ready)


def tables(owner, offsets, me):
    way, stop, train, reach, rank, slot, place = packets(owner)
    passing, ready = counts(train, reach, rank, place)
    code = schedule(passing, ready)
    used = code[:, :32] >= 0
    steps = jnp.arange(STEPS, dtype=jnp.int32)
    whole = jnp.sum(used.astype(jnp.int32)) == jnp.sum(passing[:, :32])
    needed = jnp.max(jnp.where(used, steps[:, None] + 1, 0))
    needed = jnp.where(whole, needed, STEPS + 1)
    chip, core = me // 2, me % 2

    def lane_of(way_index, back):
        at = jnp.where(way_index == 0, chip, (16 - chip) % 16)
        return way_index * 16 + (at - back + 16) % 16

    def column(index):
        return lax.dynamic_slice_in_dim(code, index, 1, 1)[:, 0]

    leaving = column(lane_of(core, 0))
    arriving = column(lane_of(core, 1))
    other = column(lane_of(1 - core, 1))
    at = jnp.where(way == 0, chip, (16 - chip) % 16)
    hops = (at - stop + 16) % 16
    mine = way == core
    local = jnp.where(owner % 2 == core, rank, 24 + rank)
    came = (hops - 1) * 64 + place
    lanes = jnp.where(mine[:, None], arriving[None, :], other[None, :])
    stored = jnp.sum(jnp.where(lanes == came[:, None], steps[None, :], 0), axis=1)
    where = jnp.where(hops == 0, local, 48 + 2 * stored + jnp.where(mine, 0, 1))
    passed = mine & (hops < reach)
    goes = jnp.where(passed, hops * 64 + place, -2)
    index = jnp.sum(jnp.where(leaving[:, None] == goes[None, :], where[None, :], 0), axis=1)
    own = owner == me
    ranks = jnp.arange(24, dtype=jnp.int32)
    order = jnp.sum(jnp.where(own[None, :] & (rank[None, :] == ranks[:, None]), slot[None, :], 0), axis=1)
    around = jnp.concatenate([where[-12:], where, where[:12]])
    location = lax.dynamic_slice_in_dim(around, me * 12, 36)
    table = jnp.concatenate([index, order, location, offsets])
    return table, needed


def wide(real, imag):
    return jnp.concatenate([real, imag], axis=1)


def main_kernel(
    size,
    table,
    weights,
    ret_hbm,
    sig_hbm,
    coupling_ref,
    out_ref,
    ret,
    sig,
    outgoing,
    lower,
    upper,
    twin,
    landed,
    relayed,
    sending,
    pool,
    left_mats,
    right_mats,
    load_sem,
    low_send,
    up_send,
    low_recv,
    up_recv,
    twin_send,
    twin_recv,
    ring_send,
    ring_recv,
    relay_send,
    relay_recv,
):
    at_order, at_location, at_offset = STEPS, STEPS + 24, STEPS + 60
    energy, slab = lax.axis_index("energy"), lax.axis_index("slab")
    core = lax.rem(energy, 2)
    step = 2 - 4 * core
    ahead = (lax.rem(energy + step + 32, 32), slab)
    behind = (lax.rem(energy - step + 32, 32), slab)
    partner = (energy + 1 - 2 * core, slab)
    slab_up = (energy, lax.rem(slab + 1, 16))
    slab_down = (energy, lax.rem(slab + 15, 16))
    has_lower = jnp.where(slab > 0, 0.5, 0.0)
    has_upper = jnp.where(slab < 15, 0.5, 0.0)

    load_sig = pltpu.make_async_copy(sig_hbm.at[0], sig, load_sem.at[0])
    load_ret = pltpu.make_async_copy(ret_hbm.at[0], ret, load_sem.at[1])
    load_sig.start()
    load_ret.start()

    barrier = pltpu.get_barrier_semaphore()
    for device in (ahead, behind, partner, slab_up, slab_down):
        pl.semaphore_signal(barrier, inc=1, device_id=device, device_id_type=MESH)

    def remote(source, target, send, receive, device):
        return pltpu.make_async_remote_copy(
            src_ref=source,
            dst_ref=target,
            send_sem=send,
            recv_sem=receive,
            device_id=device,
            device_id_type=MESH,
        )

    def to_upper(j):
        return remote(outgoing.at[j], lower.at[j], up_send.at[j], low_recv.at[j], slab_up)

    def to_lower(j):
        return remote(outgoing.at[j], upper.at[j], low_send.at[j], up_recv.at[j], slab_down)

    def to_twin(j):
        return remote(pool.at[j], twin.at[j], twin_send.at[j], twin_recv.at[j], partner)

    def to_ring(t):
        return remote(sending.at[t], landed.at[t], ring_send.at[t], ring_recv.at[t], ahead)

    def to_relay(t):
        return remote(landed.at[t], relayed.at[t], relay_send.at[t], relay_recv.at[t], partner)

    def spread(j):
        outgoing[j] = sig[table[at_order + j]]
        to_upper(j).start()
        to_lower(j).start()

    load_sig.wait()
    pl.semaphore_wait(barrier, 5)
    for j in range(AHEAD):
        spread(j)
    for k in range(4):
        m_real, m_imag = coupling_ref[k, 0], coupling_ref[k, 1]
        left_mats[k] = jnp.concatenate([wide(m_real, -m_imag), wide(m_imag, m_real)], axis=0)
        right_mats[:, 256 * k : 256 * k + 256] = jnp.concatenate(
            [wide(m_real, m_imag), wide(-m_imag, m_real)], axis=0
        )
    load_ret.wait()

    def form(j):
        to_upper(j).wait_recv()
        to_lower(j).wait_recv()
        beside = lower[j].astype(jnp.float32) * has_lower + upper[j].astype(jnp.float32) * has_upper
        total = (outgoing[j].astype(jnp.float32) + beside).astype(jnp.bfloat16)
        s_real, s_imag = total[0], total[1]
        block = ret[table[at_order + j]]
        r_real, r_imag = block[0], block[1]
        right = jnp.concatenate([wide(s_real, s_imag), wide(-s_imag, s_real)], axis=0)
        half = jnp.dot(wide(r_real, r_imag), right, preferred_element_type=jnp.float32).astype(jnp.bfloat16)
        back = jnp.concatenate([wide(r_real, r_imag), wide(-r_imag, r_real)], axis=0)
        full = lax.dot_general(half, back, (((1,), (1,)), ((), ())), preferred_element_type=jnp.float32)
        full = full.astype(jnp.bfloat16)
        pool[j, 0] = full[:, :128]
        pool[j, 1] = full[:, 128:]
        to_twin(j).start()

    def take_twin(j):
        to_twin(j).wait_recv()
        pool[24 + j] = twin[j]

    def take_ring(t):
        to_ring(t).wait_recv()
        to_relay(t).start()
        pool[48 + 2 * t] = landed[t]

    def take_relay(t):
        to_relay(t).wait_recv()
        pool[49 + 2 * t] = relayed[t]

    def send_ring(t):
        sending[t] = pool[table[t]]
        to_ring(t).start()

    def early(j, carry):
        @pl.when(j < 24 - AHEAD)
        def _():
            spread(j + AHEAD)

        form(j)

        @pl.when(j >= 1)
        def _():
            take_twin(j - 1)

        for half in (0, 1):
            t = 2 * j + half

            @pl.when(t >= LAG)
            def _():
                take_ring(t - LAG)

            send_ring(t)

            @pl.when(t >= LAG + PLAG)
            def _():
                take_relay(t - LAG - PLAG)

        return carry

    lax.fori_loop(0, 24, early, 0)
    take_twin(23)

    def late(t, carry):
        take_ring(t - LAG)
        send_ring(t)
        take_relay(t - LAG - PLAG)
        return carry

    lax.fori_loop(48, size, late, 0)

    def last(t, carry):
        take_ring(t)
        return carry

    lax.fori_loop(size - LAG, size, last, 0)

    def final(t, carry):
        take_relay(t)
        return carry

    lax.fori_loop(size - LAG - PLAG, size, final, 0)

    def weighted(i, k):
        offset = table[at_offset + k]
        up = pool[table[at_location + 12 + i + offset]].astype(jnp.float32)
        down = pool[table[at_location + 12 + i - offset]].astype(jnp.float32)
        value = (weights[k] + 1.0) * up + weights[k] * down
        return value.astype(jnp.bfloat16).reshape(256, 128)

    def finish(p, carry):
        coupled = []
        for k in range(4):
            pair = wide(weighted(2 * p, k), weighted(2 * p + 1, k))
            left = jnp.dot(left_mats[k], pair, preferred_element_type=jnp.float32).astype(jnp.bfloat16)
            rows = [wide(left[:128, c : c + 128], left[128:, c : c + 128]) for c in (0, 128)]
            coupled.append(jnp.concatenate(rows, axis=0))
        whole = jnp.concatenate(coupled, axis=1)
        result = lax.dot_general(
            whole, right_mats[...], (((1,), (1,)), ((), ())), preferred_element_type=jnp.float32
        )
        for c in (0, 1):
            out_ref[0, 2 * p + c, 0] = result[128 * c : 128 * c + 128, :128]
            out_ref[0, 2 * p + c, 1] = result[128 * c : 128 * c + 128, 128:]
        return carry

    lax.fori_loop(0, 6, finish, 0)

    def drain_x(j, carry):
        to_upper(j).wait_send()
        to_lower(j).wait_send()
        to_twin(j).wait_send()
        return carry

    lax.fori_loop(0, 24, drain_x, 0)

    def drain_z(t, carry):
        to_ring(t).wait_send()
        to_relay(t).wait_send()
        return carry

    lax.fori_loop(0, size, drain_z, 0)


def routed(size, identity, table, occupancy, retarded, self_lesser, coupling):
    def blocks(n):
        return pltpu.VMEM((n, 2, 128, 128), jnp.bfloat16)

    dma = pltpu.SemaphoreType.DMA
    return pl.pallas_call(
        functools.partial(main_kernel, size),
        out_shape=jax.ShapeDtypeStruct((1, 12, 2, 128, 128), jnp.float32),
        in_specs=[
            pl.BlockSpec(memory_space=pltpu.SMEM),
            pl.BlockSpec(memory_space=pltpu.SMEM),
            pl.BlockSpec(memory_space=pl.ANY),
            pl.BlockSpec(memory_space=pl.ANY),
            pl.BlockSpec(memory_space=pltpu.VMEM),
        ],
        out_specs=pl.BlockSpec(memory_space=pltpu.VMEM),
        scratch_shapes=[
            blocks(24),
            blocks(24),
            blocks(24),
            blocks(24),
            blocks(24),
            blocks(24),
            blocks(size),
            blocks(size),
            blocks(size),
            blocks(48 + 2 * size),
            pltpu.VMEM((4, 256, 256), jnp.bfloat16),
            pltpu.VMEM((256, 1024), jnp.bfloat16),
            dma((2,)),
            dma((24,)),
            dma((24,)),
            dma((24,)),
            dma((24,)),
            dma((24,)),
            dma((24,)),
            dma((size,)),
            dma((size,)),
            dma((size,)),
            dma((size,)),
        ],
        compiler_params=pltpu.CompilerParams(
            collective_id=identity, has_side_effects=True, vmem_limit_bytes=60 * 1024 * 1024
        ),
    )(table, occupancy, retarded, self_lesser, coupling)


def body(retarded, self_lesser, coupling, occupancy, adaptive_owner, phonon_offsets):
    me = lax.axis_index("energy")
    table, needed = tables(adaptive_owner, phonon_offsets, me)
    choice = sum((needed > size).astype(jnp.int32) for size in SIZES)

    def fast(size, identity):
        def call(_):
            return routed(size, identity, table, occupancy, retarded, self_lesser, coupling)

        return call

    def slow(_):
        return general(retarded, self_lesser, coupling, occupancy, adaptive_owner, phonon_offsets)

    branches = [fast(size, i) for i, size in enumerate(SIZES)] + [slow]
    return lax.switch(choice, branches, 0)


def solution(mesh):
    placed = (
        P("slab", "energy", None, None, None),
        P("slab", "energy", None, None, None),
        P(),
        P(),
        P(),
        P(),
    )
    return jax.shard_map(
        body,
        mesh=mesh,
        in_specs=placed,
        out_specs=P("slab", "energy", None, None, None),
        check_vma=False,
    )
```

```python
import functools

import jax
import jax.numpy as jnp
from jax import lax
from jax.experimental import pallas as pl
from jax.experimental.pallas import tpu as pltpu
from jax.sharding import PartitionSpec as P

MESH = pl.DeviceIdType.MESH
LAG = 5
START = 3
PLAG = 3
AHEAD = 6
STEPS = 110
SIZES = (88, 104)


def with_halo(array, sides, width, wrap):
    for axis, dim in sides:
        peers, length = (lax.axis_size(axis), array.shape[dim])
        up = [(i, (i + 1) % peers) for i in range(peers if wrap else peers - 1)]
        down = [(j, i) for i, j in up]
        last = lax.slice_in_dim(array, length - width, length, axis=dim)
        initial = lax.slice_in_dim(array, 0, width, axis=dim)
        before = lax.ppermute(last, axis, up)
        after = lax.ppermute(initial, axis, down)
        array = jnp.concatenate([before, array, after], axis=dim)
    return array


def batched(left_block, right_block):
    return jnp.einsum("jab,jbc->jac", left_block, right_block, preferred_element_type=jnp.float32)


def batched_transposed(left_block, right_block):
    return jnp.einsum("jab,jcb->jac", left_block, right_block, preferred_element_type=jnp.float32)


def lesser_blocks(green_ret, sigma_total):
    ret_real, ret_imag = (green_ret[:, 0], green_ret[:, 1])
    sig_real, sig_imag = (sigma_total[:, 0], sigma_total[:, 1])
    half_real = batched(ret_real, sig_real) - batched(ret_imag, sig_imag)
    half_imag = batched(ret_real, sig_imag) + batched(ret_imag, sig_real)
    half_product = jnp.stack([half_real, half_imag], 1).astype(jnp.bfloat16)
    hp_real, hp_imag = (half_product[:, 0], half_product[:, 1])
    out_real = batched_transposed(hp_real, ret_real) + batched_transposed(hp_imag, ret_imag)
    out_imag = batched_transposed(hp_imag, ret_real) - batched_transposed(hp_real, ret_imag)
    return jnp.stack([out_real, out_imag], 1).astype(jnp.bfloat16)


def combined(stacked_rims):
    own_sigma = stacked_rims[1].astype(jnp.float32)
    beside = stacked_rims[0].astype(jnp.float32) + stacked_rims[2].astype(jnp.float32)
    return (own_sigma + 0.5 * beside).astype(jnp.bfloat16)


def sandwich(coupling_mode, weighted):
    m_real, m_imag = (coupling_mode[0], coupling_mode[1])
    w_real, w_imag = (weighted[:, 0], weighted[:, 1])
    left_real = jnp.einsum(
        "ab,jbc->jac", m_real, w_real, preferred_element_type=jnp.float32
    ) - jnp.einsum("ab,jbc->jac", m_imag, w_imag, preferred_element_type=jnp.float32)
    left_imag = jnp.einsum(
        "ab,jbc->jac", m_real, w_imag, preferred_element_type=jnp.float32
    ) + jnp.einsum("ab,jbc->jac", m_imag, w_real, preferred_element_type=jnp.float32)
    coupled = jnp.stack([left_real, left_imag], 1).astype(jnp.bfloat16)
    c_real, c_imag = (coupled[:, 0], coupled[:, 1])
    out_real = jnp.einsum(
        "jab,cb->jac", c_real, m_real, preferred_element_type=jnp.float32
    ) + jnp.einsum("jab,cb->jac", c_imag, m_imag, preferred_element_type=jnp.float32)
    out_imag = jnp.einsum(
        "jab,cb->jac", c_imag, m_real, preferred_element_type=jnp.float32
    ) - jnp.einsum("jab,cb->jac", c_real, m_imag, preferred_element_type=jnp.float32)
    return jnp.stack([out_real, out_imag], 1)


def general(retarded, self_lesser, coupling, occupancy, adaptive_owner, phonon_offsets):
    n_energy = lax.axis_size("energy")
    my_index = lax.axis_index("energy")
    energies = adaptive_owner.shape[0]
    per_device = energies // n_energy
    capacity = retarded.shape[1]
    slot_count = -(-capacity // n_energy)
    positions = jnp.arange(energies, dtype=jnp.int32)
    block_of = positions // per_device
    same_owner = adaptive_owner[:, None] == adaptive_owner[None, :]
    earlier = same_owner & (positions[None, :] < positions[:, None])
    slot_rank = jnp.sum(earlier.astype(jnp.int32), axis=1)
    same_block = block_of[None, :] == block_of[:, None]
    group_rank = jnp.sum((earlier & same_block).astype(jnp.int32), axis=1)
    target = block_of * slot_count + group_rank
    targets = jnp.arange(n_energy * slot_count, dtype=jnp.int32)
    matches = (adaptive_owner == my_index)[None, :] & (target[None, :] == targets[:, None])
    send_slot = jnp.sum(jnp.where(matches, slot_rank[None, :], 0), axis=1)
    first_energy = my_index * per_device
    own_owner = lax.dynamic_slice_in_dim(adaptive_owner, first_energy, per_device)
    own_rank = lax.dynamic_slice_in_dim(group_rank, first_energy, per_device)
    receive_slot = own_owner * slot_count + own_rank
    stacked_rims = with_halo(self_lesser, (("slab", 0),), 1, False)
    formed = lesser_blocks(retarded[0], combined(stacked_rims))
    outgoing = jnp.take(formed, send_slot, axis=0)
    arrived = lax.all_to_all(outgoing, "energy", split_axis=0, concat_axis=0, tiled=True)
    lesser = jnp.take(arrived, receive_slot, axis=0)
    widened = with_halo(lesser, (("energy", 0),), per_device, True)
    accumulated = jnp.zeros((per_device, 2, lesser.shape[2], lesser.shape[3]), jnp.float32)
    for phonon_mode in range(coupling.shape[0]):
        offset = phonon_offsets[phonon_mode]
        shifted_up = lax.dynamic_slice_in_dim(widened, per_device + offset, per_device, 0).astype(
            jnp.float32
        )
        shifted_down = lax.dynamic_slice_in_dim(widened, per_device - offset, per_device, 0).astype(
            jnp.float32
        )
        weight_one = occupancy[phonon_mode]
        weighted = ((weight_one + 1.0) * shifted_up + weight_one * shifted_down).astype(
            jnp.bfloat16
        )
        accumulated = accumulated + sandwich(coupling[phonon_mode], weighted)
    return accumulated[None]


def packets(owner):
    e = jnp.arange(384, dtype=jnp.int32)
    chip, upper = owner // 2, (e // 12) % 2 == 1
    d = (e // 24 - chip + 16) % 16
    plus = jnp.where(upper, d <= 7, (d >= 1) & (d <= 8))
    there = jnp.where(upper, d + 1, d)
    back = jnp.where(upper, 16 - d, jnp.where(d == 0, 1, 17 - d))
    reach = jnp.where(plus, there, back)
    way = jnp.where(plus, 0, 1)
    stop = jnp.where(plus, chip, (16 - chip) % 16)
    train = way * 16 + stop
    key = (8 - reach) * 384 + e
    same = owner[:, None] == owner[None, :]
    before = key[None, :] < key[:, None]
    rank = jnp.sum((same & before).astype(jnp.int32), axis=1)
    slot = jnp.sum((same & (e[None, :] < e[:, None])).astype(jnp.int32), axis=1)
    place = jnp.sum(((train[:, None] == train[None, :]) & before).astype(jnp.int32), axis=1)
    return way, stop, train, reach, rank, slot, place


def counts(train, reach, rank, place):
    lane = jnp.arange(128, dtype=jnp.int32)
    hops = jnp.arange(8, dtype=jnp.int32)
    source = (lane // 16) * 16 + (lane[None, :] - hops[:, None] + 16) % 16
    through = (source[:, :, None] == train[None, None, :]) & (reach[None, None, :] > hops[:, None, None])
    passing = jnp.sum(through.astype(jnp.int32), axis=2)
    ready = jnp.arange(32, dtype=jnp.int32)
    held = (lane[None, :, None] == train[None, None, :]) & (rank[None, None, :] >= ready[:, None, None])
    first = jnp.min(jnp.where(held, place[None, None, :], 384), axis=2)
    return passing, jnp.minimum(first, passing[:1])


def schedule_kernel(passing_ref, ready_ref, code_ref, sent_ref, there_ref):
    edge = lax.broadcasted_iota(jnp.int32, (8, 128), 1) % 16 == 0
    limit = passing_ref[...]
    zero = jnp.zeros((1, 128), jnp.int32)
    for t in range(LAG):
        sent_ref[t] = jnp.zeros((8, 128), jnp.int32)

    def group(g, sent):
        for s in range(LAG):
            old = sent_ref[s]
            moved = jnp.where(edge, pltpu.roll(old, 113, 1), pltpu.roll(old, 1, 1))
            there_ref[s] = jnp.minimum(moved, limit)
        for s in range(LAG):
            t = g * LAG + s
            ready = jnp.clip((t - START + 2) // 2, 0, 24)
            code = zero - 1
            taken = zero
            out = []
            for i in range(8):
                there = ready_ref[pl.ds(ready, 1), :] if i == 0 else there_ref[s, i - 1 : i, :]
                go = jnp.where(sent[i] < there, 1 - taken, 0)
                code = jnp.where(go > 0, sent[i] + 64 * i, code)
                taken = taken + go
                out.append(sent[i] + go)
                sent_ref[s, i : i + 1, :] = out[i]
            code_ref[pl.ds(t, 1), :] = code
            sent = out
        return tuple(sent)

    lax.fori_loop(0, STEPS // LAG, group, (zero,) * 8)


def schedule(passing, ready):
    shifted = jnp.concatenate([passing[1:], passing[:1]], axis=0)
    recent = jax.ShapeDtypeStruct((LAG, 8, 128), jnp.int32)
    return pl.pallas_call(
        schedule_kernel,
        out_shape=(jax.ShapeDtypeStruct((STEPS, 128), jnp.int32), recent, recent),
        in_specs=[pl.BlockSpec(memory_space=pltpu.VMEM)] * 2,
        out_specs=(pl.BlockSpec(memory_space=pltpu.VMEM),) * 3,
    )(shifted, ready)[0]


def tables(owner, offsets, me):
    way, stop, train, reach, rank, slot, place = packets(owner)
    passing, ready = counts(train, reach, rank, place)
    code = schedule(passing, ready)
    used = code[:, :32] >= 0
    steps = jnp.arange(STEPS, dtype=jnp.int32)
    whole = jnp.sum(used.astype(jnp.int32)) == jnp.sum(passing[:, :32])
    needed = jnp.max(jnp.where(used, steps[:, None] + 1, 0))
    needed = jnp.where(whole, needed, STEPS + 1)
    chip, core = me // 2, me % 2

    def lane_of(way_index, back):
        at = jnp.where(way_index == 0, chip, (16 - chip) % 16)
        return way_index * 16 + (at - back + 16) % 16

    def column(index):
        return lax.dynamic_slice_in_dim(code, index, 1, 1)[:, 0]

    leaving = column(lane_of(core, 0))
    arriving = column(lane_of(core, 1))
    other = column(lane_of(1 - core, 1))
    at = jnp.where(way == 0, chip, (16 - chip) % 16)
    hops = (at - stop + 16) % 16
    mine = way == core
    local = jnp.where(owner % 2 == core, rank, 24 + rank)
    came = (hops - 1) * 64 + place
    lanes = jnp.where(mine[:, None], arriving[None, :], other[None, :])
    stored = jnp.sum(jnp.where(lanes == came[:, None], steps[None, :], 0), axis=1)
    where = jnp.where(hops == 0, local, 48 + 2 * stored + jnp.where(mine, 0, 1))
    passed = mine & (hops < reach)
    goes = jnp.where(passed, hops * 64 + place, -2)
    index = jnp.sum(jnp.where(leaving[:, None] == goes[None, :], where[None, :], 0), axis=1)
    own = owner == me
    ranks = jnp.arange(24, dtype=jnp.int32)
    order = jnp.sum(jnp.where(own[None, :] & (rank[None, :] == ranks[:, None]), slot[None, :], 0), axis=1)
    around = jnp.concatenate([where[-12:], where, where[:12]])
    location = lax.dynamic_slice_in_dim(around, me * 12, 36)
    table = jnp.concatenate([index, order, location, offsets])
    return table, needed


def wide(real, imag):
    return jnp.concatenate([real, imag], axis=1)


def main_kernel(
    size,
    table,
    weights,
    ret_hbm,
    sig_hbm,
    coupling_ref,
    out_ref,
    ret,
    sig,
    outgoing,
    lower,
    upper,
    twin,
    landed,
    relayed,
    sending,
    pool,
    left_mats,
    right_mats,
    load_sem,
    low_send,
    up_send,
    low_recv,
    up_recv,
    twin_send,
    twin_recv,
    ring_send,
    ring_recv,
    relay_send,
    relay_recv,
):
    at_order, at_location, at_offset = STEPS, STEPS + 24, STEPS + 60
    energy, slab = lax.axis_index("energy"), lax.axis_index("slab")
    core = lax.rem(energy, 2)
    step = 2 - 4 * core
    ahead = (lax.rem(energy + step + 32, 32), slab)
    behind = (lax.rem(energy - step + 32, 32), slab)
    partner = (energy + 1 - 2 * core, slab)
    slab_up = (energy, lax.rem(slab + 1, 16))
    slab_down = (energy, lax.rem(slab + 15, 16))
    has_lower = jnp.where(slab > 0, 0.5, 0.0)
    has_upper = jnp.where(slab < 15, 0.5, 0.0)

    load_sig = pltpu.make_async_copy(sig_hbm.at[0], sig, load_sem.at[0])
    load_ret = pltpu.make_async_copy(ret_hbm.at[0], ret, load_sem.at[1])
    load_sig.start()
    load_ret.start()

    barrier = pltpu.get_barrier_semaphore()
    for device in (ahead, behind, partner, slab_up, slab_down):
        pl.semaphore_signal(barrier, inc=1, device_id=device, device_id_type=MESH)

    def remote(source, target, send, receive, device):
        return pltpu.make_async_remote_copy(
            src_ref=source,
            dst_ref=target,
            send_sem=send,
            recv_sem=receive,
            device_id=device,
            device_id_type=MESH,
        )

    def to_upper(j):
        return remote(outgoing.at[j], lower.at[j], up_send.at[j], low_recv.at[j], slab_up)

    def to_lower(j):
        return remote(outgoing.at[j], upper.at[j], low_send.at[j], up_recv.at[j], slab_down)

    def to_twin(j):
        return remote(pool.at[j], twin.at[j], twin_send.at[j], twin_recv.at[j], partner)

    def to_ring(t):
        return remote(sending.at[t], landed.at[t], ring_send.at[t], ring_recv.at[t], ahead)

    def to_relay(t):
        return remote(landed.at[t], relayed.at[t], relay_send.at[t], relay_recv.at[t], partner)

    def spread(j):
        outgoing[j] = sig[table[at_order + j]]
        to_upper(j).start()
        to_lower(j).start()

    load_sig.wait()
    pl.semaphore_wait(barrier, 5)
    for j in range(AHEAD):
        spread(j)
    for k in range(4):
        m_real, m_imag = coupling_ref[k, 0], coupling_ref[k, 1]
        left_mats[k] = jnp.concatenate([wide(m_real, -m_imag), wide(m_imag, m_real)], axis=0)
        right_mats[:, 256 * k : 256 * k + 256] = jnp.concatenate(
            [wide(m_real, m_imag), wide(-m_imag, m_real)], axis=0
        )
    load_ret.wait()

    def form(j):
        to_upper(j).wait_recv()
        to_lower(j).wait_recv()
        beside = lower[j].astype(jnp.float32) * has_lower + upper[j].astype(jnp.float32) * has_upper
        total = (outgoing[j].astype(jnp.float32) + beside).astype(jnp.bfloat16)
        s_real, s_imag = total[0], total[1]
        block = ret[table[at_order + j]]
        r_real, r_imag = block[0], block[1]
        right = jnp.concatenate([wide(s_real, s_imag), wide(-s_imag, s_real)], axis=0)
        half = jnp.dot(wide(r_real, r_imag), right, preferred_element_type=jnp.float32).astype(jnp.bfloat16)
        back = jnp.concatenate([wide(r_real, r_imag), wide(-r_imag, r_real)], axis=0)
        full = lax.dot_general(half, back, (((1,), (1,)), ((), ())), preferred_element_type=jnp.float32)
        full = full.astype(jnp.bfloat16)
        pool[j, 0] = full[:, :128]
        pool[j, 1] = full[:, 128:]
        to_twin(j).start()

    def take_twin(j):
        to_twin(j).wait_recv()
        pool[24 + j] = twin[j]

    def take_ring(t):
        to_ring(t).wait_recv()
        to_relay(t).start()
        pool[48 + 2 * t] = landed[t]

    def take_relay(t):
        to_relay(t).wait_recv()
        pool[49 + 2 * t] = relayed[t]

    def send_ring(t):
        sending[t] = pool[table[t]]
        to_ring(t).start()

    def early(j, carry):
        @pl.when(j < 24 - AHEAD)
        def _():
            spread(j + AHEAD)

        form(j)

        @pl.when(j >= 1)
        def _():
            take_twin(j - 1)

        for half in (0, 1):
            t = 2 * j + half

            @pl.when(t >= LAG)
            def _():
                take_ring(t - LAG)

            send_ring(t)

            @pl.when(t >= LAG + PLAG)
            def _():
                take_relay(t - LAG - PLAG)

        return carry

    lax.fori_loop(0, 24, early, 0)
    take_twin(23)

    def late(t, carry):
        take_ring(t - LAG)
        send_ring(t)
        take_relay(t - LAG - PLAG)
        return carry

    lax.fori_loop(48, size, late, 0)

    def last(t, carry):
        take_ring(t)
        return carry

    lax.fori_loop(size - LAG, size, last, 0)

    def final(t, carry):
        take_relay(t)
        return carry

    lax.fori_loop(size - LAG - PLAG, size, final, 0)

    def weighted(i, k):
        offset = table[at_offset + k]
        up = pool[table[at_location + 12 + i + offset]].astype(jnp.float32)
        down = pool[table[at_location + 12 + i - offset]].astype(jnp.float32)
        value = (weights[k] + 1.0) * up + weights[k] * down
        return value.astype(jnp.bfloat16).reshape(256, 128)

    def finish(p, carry):
        coupled = []
        for k in range(4):
            pair = wide(weighted(2 * p, k), weighted(2 * p + 1, k))
            left = jnp.dot(left_mats[k], pair, preferred_element_type=jnp.float32).astype(jnp.bfloat16)
            rows = [wide(left[:128, c : c + 128], left[128:, c : c + 128]) for c in (0, 128)]
            coupled.append(jnp.concatenate(rows, axis=0))
        whole = jnp.concatenate(coupled, axis=1)
        result = lax.dot_general(
            whole, right_mats[...], (((1,), (1,)), ((), ())), preferred_element_type=jnp.float32
        )
        for c in (0, 1):
            out_ref[0, 2 * p + c, 0] = result[128 * c : 128 * c + 128, :128]
            out_ref[0, 2 * p + c, 1] = result[128 * c : 128 * c + 128, 128:]
        return carry

    lax.fori_loop(0, 6, finish, 0)

    def drain_x(j, carry):
        to_upper(j).wait_send()
        to_lower(j).wait_send()
        to_twin(j).wait_send()
        return carry

    lax.fori_loop(0, 24, drain_x, 0)

    def drain_z(t, carry):
        to_ring(t).wait_send()
        to_relay(t).wait_send()
        return carry

    lax.fori_loop(0, size, drain_z, 0)


def routed(size, identity, table, occupancy, retarded, self_lesser, coupling):
    def blocks(n):
        return pltpu.VMEM((n, 2, 128, 128), jnp.bfloat16)

    dma = pltpu.SemaphoreType.DMA
    return pl.pallas_call(
        functools.partial(main_kernel, size),
        out_shape=jax.ShapeDtypeStruct((1, 12, 2, 128, 128), jnp.float32),
        in_specs=[
            pl.BlockSpec(memory_space=pltpu.SMEM),
            pl.BlockSpec(memory_space=pltpu.SMEM),
            pl.BlockSpec(memory_space=pl.ANY),
            pl.BlockSpec(memory_space=pl.ANY),
            pl.BlockSpec(memory_space=pltpu.VMEM),
        ],
        out_specs=pl.BlockSpec(memory_space=pltpu.VMEM),
        scratch_shapes=[
            blocks(24),
            blocks(24),
            blocks(24),
            blocks(24),
            blocks(24),
            blocks(24),
            blocks(size),
            blocks(size),
            blocks(size),
            blocks(48 + 2 * size),
            pltpu.VMEM((4, 256, 256), jnp.bfloat16),
            pltpu.VMEM((256, 1024), jnp.bfloat16),
            dma((2,)),
            dma((24,)),
            dma((24,)),
            dma((24,)),
            dma((24,)),
            dma((24,)),
            dma((24,)),
            dma((size,)),
            dma((size,)),
            dma((size,)),
            dma((size,)),
        ],
        compiler_params=pltpu.CompilerParams(
            collective_id=identity, has_side_effects=True, vmem_limit_bytes=60 * 1024 * 1024
        ),
    )(table, occupancy, retarded, self_lesser, coupling)


def body(retarded, self_lesser, coupling, occupancy, adaptive_owner, phonon_offsets):
    me = lax.axis_index("energy")
    table, needed = tables(adaptive_owner, phonon_offsets, me)
    choice = sum((needed > size).astype(jnp.int32) for size in SIZES)

    def fast(size, identity):
        def call(_):
            return routed(size, identity, table, occupancy, retarded, self_lesser, coupling)

        return call

    def slow(_):
        return general(retarded, self_lesser, coupling, occupancy, adaptive_owner, phonon_offsets)

    branches = [fast(size, i) for i, size in enumerate(SIZES)] + [slow]
    return lax.switch(choice, branches, 0)


def solution(mesh):
    placed = (
        P("slab", "energy", None, None, None),
        P("slab", "energy", None, None, None),
        P(),
        P(),
        P(),
        P(),
    )
    return jax.shard_map(
        body,
        mesh=mesh,
        in_specs=placed,
        out_specs=P("slab", "energy", None, None, None),
        check_vma=False,
    )
```

```python
import functools

import jax
import jax.numpy as jnp
from jax import lax
from jax.experimental import pallas as pl
from jax.experimental.pallas import tpu as pltpu
from jax.sharding import PartitionSpec as P

MESH = pl.DeviceIdType.MESH
LAG = 5
PLAG = 3
AHEAD = 12
STEPS = 110
SIZES = (76, 84, 108)


def with_halo(array, sides, width, wrap):
    for axis, dim in sides:
        peers, length = (lax.axis_size(axis), array.shape[dim])
        up = [(i, (i + 1) % peers) for i in range(peers if wrap else peers - 1)]
        down = [(j, i) for i, j in up]
        last = lax.slice_in_dim(array, length - width, length, axis=dim)
        initial = lax.slice_in_dim(array, 0, width, axis=dim)
        before = lax.ppermute(last, axis, up)
        after = lax.ppermute(initial, axis, down)
        array = jnp.concatenate([before, array, after], axis=dim)
    return array


def batched(left_block, right_block):
    return jnp.einsum("jab,jbc->jac", left_block, right_block, preferred_element_type=jnp.float32)


def batched_transposed(left_block, right_block):
    return jnp.einsum("jab,jcb->jac", left_block, right_block, preferred_element_type=jnp.float32)


def lesser_blocks(green_ret, sigma_total):
    ret_real, ret_imag = (green_ret[:, 0], green_ret[:, 1])
    sig_real, sig_imag = (sigma_total[:, 0], sigma_total[:, 1])
    half_real = batched(ret_real, sig_real) - batched(ret_imag, sig_imag)
    half_imag = batched(ret_real, sig_imag) + batched(ret_imag, sig_real)
    half_product = jnp.stack([half_real, half_imag], 1).astype(jnp.bfloat16)
    hp_real, hp_imag = (half_product[:, 0], half_product[:, 1])
    out_real = batched_transposed(hp_real, ret_real) + batched_transposed(hp_imag, ret_imag)
    out_imag = batched_transposed(hp_imag, ret_real) - batched_transposed(hp_real, ret_imag)
    return jnp.stack([out_real, out_imag], 1).astype(jnp.bfloat16)


def combined(stacked_rims):
    own_sigma = stacked_rims[1].astype(jnp.float32)
    beside = stacked_rims[0].astype(jnp.float32) + stacked_rims[2].astype(jnp.float32)
    return (own_sigma + 0.5 * beside).astype(jnp.bfloat16)


def sandwich(coupling_mode, weighted):
    m_real, m_imag = (coupling_mode[0], coupling_mode[1])
    w_real, w_imag = (weighted[:, 0], weighted[:, 1])
    left_real = jnp.einsum(
        "ab,jbc->jac", m_real, w_real, preferred_element_type=jnp.float32
    ) - jnp.einsum("ab,jbc->jac", m_imag, w_imag, preferred_element_type=jnp.float32)
    left_imag = jnp.einsum(
        "ab,jbc->jac", m_real, w_imag, preferred_element_type=jnp.float32
    ) + jnp.einsum("ab,jbc->jac", m_imag, w_real, preferred_element_type=jnp.float32)
    coupled = jnp.stack([left_real, left_imag], 1).astype(jnp.bfloat16)
    c_real, c_imag = (coupled[:, 0], coupled[:, 1])
    out_real = jnp.einsum(
        "jab,cb->jac", c_real, m_real, preferred_element_type=jnp.float32
    ) + jnp.einsum("jab,cb->jac", c_imag, m_imag, preferred_element_type=jnp.float32)
    out_imag = jnp.einsum(
        "jab,cb->jac", c_imag, m_real, preferred_element_type=jnp.float32
    ) - jnp.einsum("jab,cb->jac", c_real, m_imag, preferred_element_type=jnp.float32)
    return jnp.stack([out_real, out_imag], 1)


def general(retarded, self_lesser, coupling, occupancy, adaptive_owner, phonon_offsets):
    n_energy = lax.axis_size("energy")
    my_index = lax.axis_index("energy")
    energies = adaptive_owner.shape[0]
    per_device = energies // n_energy
    capacity = retarded.shape[1]
    slot_count = -(-capacity // n_energy)
    positions = jnp.arange(energies, dtype=jnp.int32)
    block_of = positions // per_device
    same_owner = adaptive_owner[:, None] == adaptive_owner[None, :]
    earlier = same_owner & (positions[None, :] < positions[:, None])
    slot_rank = jnp.sum(earlier.astype(jnp.int32), axis=1)
    same_block = block_of[None, :] == block_of[:, None]
    group_rank = jnp.sum((earlier & same_block).astype(jnp.int32), axis=1)
    target = block_of * slot_count + group_rank
    targets = jnp.arange(n_energy * slot_count, dtype=jnp.int32)
    matches = (adaptive_owner == my_index)[None, :] & (target[None, :] == targets[:, None])
    send_slot = jnp.sum(jnp.where(matches, slot_rank[None, :], 0), axis=1)
    first_energy = my_index * per_device
    own_owner = lax.dynamic_slice_in_dim(adaptive_owner, first_energy, per_device)
    own_rank = lax.dynamic_slice_in_dim(group_rank, first_energy, per_device)
    receive_slot = own_owner * slot_count + own_rank
    stacked_rims = with_halo(self_lesser, (("slab", 0),), 1, False)
    formed = lesser_blocks(retarded[0], combined(stacked_rims))
    outgoing = jnp.take(formed, send_slot, axis=0)
    arrived = lax.all_to_all(outgoing, "energy", split_axis=0, concat_axis=0, tiled=True)
    lesser = jnp.take(arrived, receive_slot, axis=0)
    widened = with_halo(lesser, (("energy", 0),), per_device, True)
    accumulated = jnp.zeros((per_device, 2, lesser.shape[2], lesser.shape[3]), jnp.float32)
    for phonon_mode in range(coupling.shape[0]):
        offset = phonon_offsets[phonon_mode]
        shifted_up = lax.dynamic_slice_in_dim(widened, per_device + offset, per_device, 0).astype(
            jnp.float32
        )
        shifted_down = lax.dynamic_slice_in_dim(widened, per_device - offset, per_device, 0).astype(
            jnp.float32
        )
        weight_one = occupancy[phonon_mode]
        weighted = ((weight_one + 1.0) * shifted_up + weight_one * shifted_down).astype(
            jnp.bfloat16
        )
        accumulated = accumulated + sandwich(coupling[phonon_mode], weighted)
    return accumulated[None]


def tree(combine, values):
    while len(values) > 1:
        pairs = [combine(a, b) for a, b in zip(values[::2], values[1::2])]
        values = pairs + ([values[-1]] if len(values) % 2 else [])
    return values[0]


def route_kernel(me_of, owner_ref, table_ref, code_ref, limit_ref, ready_ref, count_ref, recent_ref, there_ref):
    f32 = jnp.float32
    me = me_of()

    def real(value):
        return value.astype(f32)

    def one(mask):
        return jnp.where(mask, 1.0, 0.0)

    owner = owner_ref[...].reshape(1, 384)
    e = lax.broadcasted_iota(jnp.int32, (1, 384), 1)
    uniform = ((real(e) + 0.5) * (1.0 / 12.0)).astype(jnp.int32)
    chip, upper = owner // 2, uniform % 2
    d = (uniform // 2 - chip) & 15
    up = upper == 1
    plus = jnp.where(up, jnp.where(d <= 7, 1, 0), jnp.where((d >= 1) & (d <= 8), 1, 0)) == 1
    there = d + upper
    back = jnp.where(up, 16 - d, jnp.where(d == 0, 1, 17 - d))
    reach = jnp.where(plus, there, back)
    way = jnp.where(plus, 0, 1)
    stop = jnp.where(plus, chip, (16 - chip) & 15)
    train = way * 16 + stop
    key = (8 - reach) * 384 + e

    zero_row = jnp.zeros((1, 384), f32)
    direct = jnp.where(owner % 2 == way, 1.0, 0.0)
    rows = [real(owner), real(key), real(train), real(reach), real(e), direct, zero_row, zero_row]
    columns = jnp.transpose(jnp.concatenate(rows, axis=0))
    rank, slot, place = zero_row, zero_row, zero_row
    for c in range(0, 384, 32):
        part = columns[c : c + 32]
        same = part[:, 0:1] == rows[0]
        before = part[:, 1:2] < rows[1]
        rank = rank + jnp.sum(one(same & before), axis=0, keepdims=True)
        slot = slot + jnp.sum(one(same & (part[:, 4:5] < rows[4])), axis=0, keepdims=True)
        place = place + jnp.sum(one((part[:, 2:3] == rows[2]) & before), axis=0, keepdims=True)
    ranked = jnp.transpose(jnp.concatenate([rank, place] + [zero_row] * 6, axis=0))

    lane = lax.broadcasted_iota(jnp.int32, (1, 128), 1)
    quarter, link = lane // 32, lane % 32
    passing = [jnp.zeros((1, 128), f32) for _ in range(2)]
    ready = [[jnp.full((1, 128), 384.0, f32) for _ in range(7)] for _ in range(2)]
    for c in range(0, 384, 32):
        part, more = columns[c : c + 32], ranked[c : c + 32]
        held = part[:, 2:3] == real(link)
        for h in (0, 1):
            through = held & (part[:, 3:4] > real(quarter + 4 * h))
            passing[h] = passing[h] + jnp.sum(one(through), axis=0, keepdims=True)
        for kind in (0, 1):
            mine = jnp.where(held & (part[:, 5:6] == 1.0 - kind), more[:, 1:2], 384.0)
            for h in range(7):
                first = jnp.where(more[:, 0:1] >= real(quarter + 4 * h), mine, 384.0)
                ready[kind][h] = jnp.minimum(ready[kind][h], jnp.min(first, axis=0, keepdims=True))

    def split(vector):
        return [vector] + [pltpu.roll(vector, 128 - 32 * g, 1) for g in (1, 2, 3)]

    def moved(vector, hops):
        return jnp.where(lane % 16 >= hops, pltpu.roll(vector, hops, 1), pltpu.roll(vector, 112 + hops, 1))

    totals = split(passing[0]) + split(passing[1])
    total = jnp.sum(jnp.where(lane < 32, sum(totals), 0.0))
    place_of = {}
    for i in range(8):
        for v in range(i, 8):
            place_of[i, v] = len(place_of)
            row = moved(totals[v], i) if i else totals[v]
            count_ref[place_of[i, v] : place_of[i, v] + 1, :] = row
            if i == v and i:
                limit_ref[i - 1 : i, :] = row
    limit_ref[7:8, :] = totals[0]
    for kind in (0, 1):
        for h in range(7):
            for g, row in enumerate(split(ready[kind][h])):
                at = 32 * kind + 4 * h + g
                ready_ref[at : at + 1, :] = jnp.minimum(row, totals[0])

    edge = lax.broadcasted_iota(jnp.int32, (8, 128), 1) % 16 == 0
    zero = jnp.zeros((1, 128), f32)
    for t in range(LAG):
        recent_ref[t] = jnp.zeros((8, 128), f32)
    code_ref[STEPS : STEPS + 2, :] = jnp.full((2, 128), -1.0, f32)
    limit = limit_ref[...]

    def group(g, sent):
        for s in range(LAG):
            old = recent_ref[s]
            came = jnp.where(edge, pltpu.roll(old, 113, 1), pltpu.roll(old, 1, 1))
            there_ref[s] = jnp.minimum(came, limit)
        for s in range(LAG):
            t = g * LAG + s
            direct = jnp.minimum(2 * (t // 5) + 1 + jnp.where(t % 5 >= 2, 1, 0), 24)
            via_twin = jnp.minimum(2 * (t // 5) + jnp.where(t % 5 >= 3, 1, 0), 24)
            scores = []
            for i in range(8):
                if i == 0:
                    most = jnp.minimum(ready_ref[pl.ds(direct, 1), :], ready_ref[pl.ds(32 + via_twin, 1), :])
                else:
                    most = there_ref[s, i - 1 : i, :]
                ahead = [
                    jnp.where(sent[i] < count_ref[place_of[i, v] : place_of[i, v] + 1, :], 8.0, 0.0)
                    for v in range(i, 8)
                ]
                scores.append(jnp.where(sent[i] < most, tree(jnp.add, ahead) + (7.0 - i), 0.0))
            best = jnp.maximum(tree(jnp.maximum, scores), 1.0)
            go = [jnp.where(score == best, 1.0, 0.0) for score in scores]
            code_ref[pl.ds(t, 1), :] = tree(jnp.add, [go[i] * (sent[i] + (64.0 * i + 1.0)) for i in range(8)]) - 1.0
            sent = [sent[i] + go[i] for i in range(8)]
            for i in range(8):
                recent_ref[s, i : i + 1, :] = sent[i]
        return tuple(sent)

    lax.fori_loop(0, STEPS // LAG, group, (zero,) * 8)

    code = code_ref[...]
    lanes = lax.broadcasted_iota(jnp.int32, (STEPS + 2, 128), 1)
    slots = real(lax.broadcasted_iota(jnp.int32, (STEPS + 2, 1), 0))
    used = (code >= 0.0) & (lanes < 32)
    sent_all = jnp.sum(one(used))
    needed = jnp.max(jnp.where(used, slots + 1.0, 0.0))
    needed = jnp.where(sent_all == total, needed, STEPS + 1.0)
    core, home = me % 2, me // 2
    mirror = (16 - home) & 15
    at = jnp.where(core == 0, home, mirror)
    twin_at = jnp.where(core == 0, mirror, home)

    def column(index):
        return jnp.sum(jnp.where(lanes == index, code, 0.0), axis=1, keepdims=True)

    leaving = column(core * 16 + at)
    arriving = column(core * 16 + ((at + 15) & 15))
    other = column((1 - core) * 16 + ((twin_at + 15) & 15))
    hops = (jnp.where(plus, home, mirror) - stop) & 15
    mine = way == core
    local = jnp.where(owner % 2 == core, rank, 24.0 + rank)
    came = real(hops - 1) * 64.0 + place
    stored = jnp.sum(jnp.where(arriving == came, 2.0 * slots, 0.0), axis=0, keepdims=True)
    relayed = jnp.sum(jnp.where(other == came, 2.0 * slots, 0.0), axis=0, keepdims=True)
    where = jnp.where(hops == 0, local, jnp.where(mine, 48.0 + stored, 49.0 + relayed))
    goes = jnp.where(mine & (hops < reach), real(hops) * 64.0 + place, -2.0)
    index = jnp.sum(jnp.where(leaving == goes, where, 0.0), axis=1, keepdims=True)
    ranks = real(lax.broadcasted_iota(jnp.int32, (24, 1), 0))
    order = jnp.sum(jnp.where((owner == me) & (rank == ranks), slot, 0.0), axis=1, keepdims=True)
    wanted = lax.broadcasted_iota(jnp.int32, (40, 1), 0) + 12 * me - 12
    wanted = jnp.where(wanted < 0, wanted + 384, jnp.where(wanted >= 384, wanted - 384, wanted))
    location = jnp.sum(jnp.where(wanted == e, where, 0.0), axis=1, keepdims=True)
    first = jnp.concatenate([index, jnp.zeros((128 - STEPS - 2, 1), f32)], axis=0)
    second = jnp.concatenate([order, location, jnp.full((8, 1), needed, f32), jnp.zeros((56, 1), f32)], axis=0)
    for r, part in enumerate((first, second)):
        whole = jnp.transpose(jnp.broadcast_to(part, (128, 128)))
        table_ref[r : r + 1, :] = whole[0:1].astype(jnp.int32)


def tables(owner, me_of):
    def area(*shape):
        return jax.ShapeDtypeStruct(shape, jnp.float32)

    def kernel(*refs):
        route_kernel(me_of, *refs)

    return pl.pallas_call(
        kernel,
        out_shape=(
            jax.ShapeDtypeStruct((2, 128), jnp.int32),
            area(STEPS + 2, 128),
            area(8, 128),
            area(64, 128),
            area(40, 128),
            area(LAG, 8, 128),
            area(LAG, 8, 128),
        ),
        in_specs=[pl.BlockSpec(memory_space=pltpu.VMEM)],
        out_specs=(pl.BlockSpec(memory_space=pltpu.VMEM),) * 7,
    )(owner)[0]


def wide(real, imag):
    return jnp.concatenate([real, imag], axis=1)


def main_kernel(
    size,
    table,
    weights,
    offsets,
    ret_hbm,
    sig_hbm,
    coupling_ref,
    out_ref,
    ret,
    sig,
    outgoing,
    lower,
    upper,
    twin,
    landed,
    relayed,
    sending,
    pool,
    left_mats,
    right_mats,
    load_sem,
    low_send,
    up_send,
    low_recv,
    up_recv,
    twin_send,
    twin_recv,
    ring_send,
    ring_recv,
    relay_send,
    relay_recv,
):
    energy, slab = lax.axis_index("energy"), lax.axis_index("slab")
    core = lax.rem(energy, 2)
    step = 2 - 4 * core
    ahead = (lax.rem(energy + step + 32, 32), slab)
    behind = (lax.rem(energy - step + 32, 32), slab)
    partner = (energy + 1 - 2 * core, slab)
    slab_up = (energy, lax.rem(slab + 1, 16))
    slab_down = (energy, lax.rem(slab + 15, 16))
    has_lower = jnp.where(slab > 0, 0.5, 0.0)
    has_upper = jnp.where(slab < 15, 0.5, 0.0)

    load_sig = pltpu.make_async_copy(sig_hbm.at[0], sig, load_sem.at[0])
    load_ret = pltpu.make_async_copy(ret_hbm.at[0], ret, load_sem.at[1])
    load_sig.start()
    load_ret.start()

    barrier = pltpu.get_barrier_semaphore()
    for device in (ahead, behind, partner, slab_up, slab_down):
        pl.semaphore_signal(barrier, inc=1, device_id=device, device_id_type=MESH)

    def remote(source, target, send, receive, device):
        return pltpu.make_async_remote_copy(
            src_ref=source,
            dst_ref=target,
            send_sem=send,
            recv_sem=receive,
            device_id=device,
            device_id_type=MESH,
        )

    def to_upper(j):
        return remote(outgoing.at[j], lower.at[j], up_send.at[j], low_recv.at[j], slab_up)

    def to_lower(j):
        return remote(outgoing.at[j], upper.at[j], low_send.at[j], up_recv.at[j], slab_down)

    def to_twin(j):
        return remote(pool.at[j], twin.at[j], twin_send.at[j], twin_recv.at[j], partner)

    def to_ring(t):
        return remote(sending.at[t], landed.at[t], ring_send.at[t], ring_recv.at[t], ahead)

    def to_relay(t):
        return remote(landed.at[t], relayed.at[t], relay_send.at[t], relay_recv.at[t], partner)

    def spread(j):
        outgoing[j] = sig[table[1, j]]
        to_upper(j).start()
        to_lower(j).start()

    load_sig.wait()
    pl.semaphore_wait(barrier, 5)
    for j in range(AHEAD):
        spread(j)
    for k in range(4):
        m_real, m_imag = coupling_ref[k, 0], coupling_ref[k, 1]
        left_mats[k] = jnp.concatenate([wide(m_real, -m_imag), wide(m_imag, m_real)], axis=0)
        right_mats[:, 256 * k : 256 * k + 256] = jnp.concatenate(
            [wide(m_real, m_imag), wide(-m_imag, m_real)], axis=0
        )
    load_ret.wait()

    def form(j):
        to_upper(j).wait_recv()
        to_lower(j).wait_recv()
        beside = lower[j].astype(jnp.float32) * has_lower + upper[j].astype(jnp.float32) * has_upper
        total = (outgoing[j].astype(jnp.float32) + beside).astype(jnp.bfloat16)
        s_real, s_imag = total[0], total[1]
        block = ret[table[1, j]]
        r_real, r_imag = block[0], block[1]
        right = jnp.concatenate([wide(s_real, s_imag), wide(-s_imag, s_real)], axis=0)
        half = jnp.dot(wide(r_real, r_imag), right, preferred_element_type=jnp.float32).astype(jnp.bfloat16)
        back = jnp.concatenate([wide(r_real, r_imag), wide(-r_imag, r_real)], axis=0)
        full = lax.dot_general(half, back, (((1,), (1,)), ((), ())), preferred_element_type=jnp.float32)
        full = full.astype(jnp.bfloat16)
        pool[j, 0] = full[:, :128]
        pool[j, 1] = full[:, 128:]
        to_twin(j).start()

    def take_twin(j):
        to_twin(j).wait_recv()
        pool[24 + j] = twin[j]

    def take_ring(t):
        to_ring(t).wait_recv()
        to_relay(t).start()
        pool[48 + 2 * t] = landed[t]
        to_ring(t).wait_send()

    def take_relay(t):
        to_relay(t).wait_recv()
        pool[49 + 2 * t] = relayed[t]
        to_relay(t).wait_send()

    def send_ring(t):
        sending[t] = pool[table[0, t]]
        to_ring(t).start()

    def early(g, carry):
        def ring(k):
            t = 5 * g + k

            @pl.when(t >= LAG)
            def _():
                take_ring(t - LAG)

            send_ring(t)

            @pl.when(t >= LAG + PLAG)
            def _():
                take_relay(t - LAG - PLAG)

        @pl.when(g < (24 - AHEAD) // 2)
        def _():
            spread(2 * g + AHEAD)
            spread(2 * g + AHEAD + 1)

        form(2 * g)

        @pl.when(g >= 1)
        def _():
            take_twin(2 * g - 1)

        ring(0)
        ring(1)
        form(2 * g + 1)
        ring(2)
        take_twin(2 * g)
        ring(3)
        ring(4)
        return carry

    lax.fori_loop(0, 12, early, 0)
    take_twin(23)

    def late(t, carry):
        take_ring(t - LAG)
        send_ring(t)
        take_relay(t - LAG - PLAG)
        return carry

    lax.fori_loop(60, size, late, 0)

    def drain(j, carry):
        to_upper(j).wait_send()
        to_lower(j).wait_send()
        to_twin(j).wait_send()
        return carry

    lax.fori_loop(0, 24, drain, 0)

    def last(t, carry):
        take_ring(t)
        take_relay(t - PLAG)
        return carry

    lax.fori_loop(size - LAG, size, last, 0)

    def final(t, carry):
        take_relay(t)
        return carry

    lax.fori_loop(size - PLAG, size, final, 0)

    def weighted(i, k):
        offset = offsets[k]
        up = pool[table[1, 36 + i + offset]].astype(jnp.float32)
        down = pool[table[1, 36 + i - offset]].astype(jnp.float32)
        value = (weights[k] + 1.0) * up + weights[k] * down
        return value.astype(jnp.bfloat16).reshape(256, 128)

    def finish(p, carry):
        coupled = []
        for k in range(4):
            pair = wide(weighted(2 * p, k), weighted(2 * p + 1, k))
            left = jnp.dot(left_mats[k], pair, preferred_element_type=jnp.float32).astype(jnp.bfloat16)
            rows = [wide(left[:128, c : c + 128], left[128:, c : c + 128]) for c in (0, 128)]
            coupled.append(jnp.concatenate(rows, axis=0))
        whole = jnp.concatenate(coupled, axis=1)
        result = lax.dot_general(
            whole, right_mats[...], (((1,), (1,)), ((), ())), preferred_element_type=jnp.float32
        )
        for c in (0, 1):
            out_ref[0, 2 * p + c, 0] = result[128 * c : 128 * c + 128, :128]
            out_ref[0, 2 * p + c, 1] = result[128 * c : 128 * c + 128, 128:]
        return carry

    lax.fori_loop(0, 6, finish, 0, unroll=2)


def routed(size, identity, table, occupancy, offsets, retarded, self_lesser, coupling):
    def blocks(n):
        return pltpu.VMEM((n, 2, 128, 128), jnp.bfloat16)

    dma = pltpu.SemaphoreType.DMA
    return pl.pallas_call(
        functools.partial(main_kernel, size),
        out_shape=jax.ShapeDtypeStruct((1, 12, 2, 128, 128), jnp.float32),
        in_specs=[
            pl.BlockSpec(memory_space=pltpu.SMEM),
            pl.BlockSpec(memory_space=pltpu.SMEM),
            pl.BlockSpec(memory_space=pltpu.SMEM),
            pl.BlockSpec(memory_space=pl.ANY),
            pl.BlockSpec(memory_space=pl.ANY),
            pl.BlockSpec(memory_space=pltpu.VMEM),
        ],
        out_specs=pl.BlockSpec(memory_space=pltpu.VMEM),
        scratch_shapes=[
            blocks(24),
            blocks(24),
            blocks(24),
            blocks(24),
            blocks(24),
            blocks(24),
            blocks(size),
            blocks(size),
            blocks(size),
            blocks(48 + 2 * size),
            pltpu.VMEM((4, 256, 256), jnp.bfloat16),
            pltpu.VMEM((256, 1024), jnp.bfloat16),
            dma((2,)),
            dma((24,)),
            dma((24,)),
            dma((24,)),
            dma((24,)),
            dma((24,)),
            dma((24,)),
            dma((size,)),
            dma((size,)),
            dma((size,)),
            dma((size,)),
        ],
        compiler_params=pltpu.CompilerParams(
            collective_id=identity, has_side_effects=True, vmem_limit_bytes=60 * 1024 * 1024
        ),
    )(table, occupancy, offsets, retarded, self_lesser, coupling)


def body(retarded, self_lesser, coupling, occupancy, adaptive_owner, phonon_offsets):
    table = tables(adaptive_owner, lambda: lax.axis_index("energy"))
    needed = table[1, 64]
    choice = sum((needed > size).astype(jnp.int32) for size in SIZES)

    def fast(size, identity):
        def call(_):
            return routed(size, identity, table, occupancy, phonon_offsets, retarded, self_lesser, coupling)

        return call

    def slow(_):
        return general(retarded, self_lesser, coupling, occupancy, adaptive_owner, phonon_offsets)

    branches = [fast(size, i) for i, size in enumerate(SIZES)] + [slow]
    return lax.switch(choice, branches, 0)


def solution(mesh):
    placed = (
        P("slab", "energy", None, None, None),
        P("slab", "energy", None, None, None),
        P(),
        P(),
        P(),
        P(),
    )
    return jax.shard_map(
        body,
        mesh=mesh,
        in_specs=placed,
        out_specs=P("slab", "energy", None, None, None),
        check_vma=False,
    )
```

```python
import functools

import jax
import jax.numpy as jnp
from jax import lax
from jax.experimental import pallas as pl
from jax.experimental.pallas import tpu as pltpu
from jax.sharding import PartitionSpec as P

MESH = pl.DeviceIdType.MESH
LAG = 5
FLIGHT = 10
PLAG = 3
AHEAD = 12
STEPS = 105
ROWS = 112
SIZES = (74, 80, 86, 104)


def with_halo(array, sides, width, wrap):
    for axis, dim in sides:
        peers, length = (lax.axis_size(axis), array.shape[dim])
        up = [(i, (i + 1) % peers) for i in range(peers if wrap else peers - 1)]
        down = [(j, i) for i, j in up]
        last = lax.slice_in_dim(array, length - width, length, axis=dim)
        initial = lax.slice_in_dim(array, 0, width, axis=dim)
        before = lax.ppermute(last, axis, up)
        after = lax.ppermute(initial, axis, down)
        array = jnp.concatenate([before, array, after], axis=dim)
    return array


def batched(left_block, right_block):
    return jnp.einsum("jab,jbc->jac", left_block, right_block, preferred_element_type=jnp.float32)


def batched_transposed(left_block, right_block):
    return jnp.einsum("jab,jcb->jac", left_block, right_block, preferred_element_type=jnp.float32)


def lesser_blocks(green_ret, sigma_total):
    ret_real, ret_imag = (green_ret[:, 0], green_ret[:, 1])
    sig_real, sig_imag = (sigma_total[:, 0], sigma_total[:, 1])
    half_real = batched(ret_real, sig_real) - batched(ret_imag, sig_imag)
    half_imag = batched(ret_real, sig_imag) + batched(ret_imag, sig_real)
    half_product = jnp.stack([half_real, half_imag], 1).astype(jnp.bfloat16)
    hp_real, hp_imag = (half_product[:, 0], half_product[:, 1])
    out_real = batched_transposed(hp_real, ret_real) + batched_transposed(hp_imag, ret_imag)
    out_imag = batched_transposed(hp_imag, ret_real) - batched_transposed(hp_real, ret_imag)
    return jnp.stack([out_real, out_imag], 1).astype(jnp.bfloat16)


def combined(stacked_rims):
    own_sigma = stacked_rims[1].astype(jnp.float32)
    beside = stacked_rims[0].astype(jnp.float32) + stacked_rims[2].astype(jnp.float32)
    return (own_sigma + 0.5 * beside).astype(jnp.bfloat16)


def sandwich(coupling_mode, weighted):
    m_real, m_imag = (coupling_mode[0], coupling_mode[1])
    w_real, w_imag = (weighted[:, 0], weighted[:, 1])
    left_real = jnp.einsum(
        "ab,jbc->jac", m_real, w_real, preferred_element_type=jnp.float32
    ) - jnp.einsum("ab,jbc->jac", m_imag, w_imag, preferred_element_type=jnp.float32)
    left_imag = jnp.einsum(
        "ab,jbc->jac", m_real, w_imag, preferred_element_type=jnp.float32
    ) + jnp.einsum("ab,jbc->jac", m_imag, w_real, preferred_element_type=jnp.float32)
    coupled = jnp.stack([left_real, left_imag], 1).astype(jnp.bfloat16)
    c_real, c_imag = (coupled[:, 0], coupled[:, 1])
    out_real = jnp.einsum(
        "jab,cb->jac", c_real, m_real, preferred_element_type=jnp.float32
    ) + jnp.einsum("jab,cb->jac", c_imag, m_imag, preferred_element_type=jnp.float32)
    out_imag = jnp.einsum(
        "jab,cb->jac", c_imag, m_real, preferred_element_type=jnp.float32
    ) - jnp.einsum("jab,cb->jac", c_real, m_imag, preferred_element_type=jnp.float32)
    return jnp.stack([out_real, out_imag], 1)


def general(retarded, self_lesser, coupling, occupancy, adaptive_owner, phonon_offsets):
    n_energy = lax.axis_size("energy")
    my_index = lax.axis_index("energy")
    energies = adaptive_owner.shape[0]
    per_device = energies // n_energy
    capacity = retarded.shape[1]
    slot_count = -(-capacity // n_energy)
    positions = jnp.arange(energies, dtype=jnp.int32)
    block_of = positions // per_device
    same_owner = adaptive_owner[:, None] == adaptive_owner[None, :]
    earlier = same_owner & (positions[None, :] < positions[:, None])
    slot_rank = jnp.sum(earlier.astype(jnp.int32), axis=1)
    same_block = block_of[None, :] == block_of[:, None]
    group_rank = jnp.sum((earlier & same_block).astype(jnp.int32), axis=1)
    target = block_of * slot_count + group_rank
    targets = jnp.arange(n_energy * slot_count, dtype=jnp.int32)
    matches = (adaptive_owner == my_index)[None, :] & (target[None, :] == targets[:, None])
    send_slot = jnp.sum(jnp.where(matches, slot_rank[None, :], 0), axis=1)
    first_energy = my_index * per_device
    own_owner = lax.dynamic_slice_in_dim(adaptive_owner, first_energy, per_device)
    own_rank = lax.dynamic_slice_in_dim(group_rank, first_energy, per_device)
    receive_slot = own_owner * slot_count + own_rank
    stacked_rims = with_halo(self_lesser, (("slab", 0),), 1, False)
    formed = lesser_blocks(retarded[0], combined(stacked_rims))
    outgoing = jnp.take(formed, send_slot, axis=0)
    arrived = lax.all_to_all(outgoing, "energy", split_axis=0, concat_axis=0, tiled=True)
    lesser = jnp.take(arrived, receive_slot, axis=0)
    widened = with_halo(lesser, (("energy", 0),), per_device, True)
    accumulated = jnp.zeros((per_device, 2, lesser.shape[2], lesser.shape[3]), jnp.float32)
    for phonon_mode in range(coupling.shape[0]):
        offset = phonon_offsets[phonon_mode]
        shifted_up = lax.dynamic_slice_in_dim(widened, per_device + offset, per_device, 0).astype(
            jnp.float32
        )
        shifted_down = lax.dynamic_slice_in_dim(widened, per_device - offset, per_device, 0).astype(
            jnp.float32
        )
        weight_one = occupancy[phonon_mode]
        weighted = ((weight_one + 1.0) * shifted_up + weight_one * shifted_down).astype(
            jnp.bfloat16
        )
        accumulated = accumulated + sandwich(coupling[phonon_mode], weighted)
    return accumulated[None]


def tree(combine, values):
    while len(values) > 1:
        pairs = [combine(a, b) for a, b in zip(values[::2], values[1::2])]
        values = pairs + ([values[-1]] if len(values) % 2 else [])
    return values[0]


def route_kernel(me_of, owner_ref, table_ref, code_ref, limit_ref, ready_ref, count_ref, recent_ref, there_ref):
    f32 = jnp.float32
    me = me_of()

    def real(value):
        return value.astype(f32)

    def one(mask):
        return jnp.where(mask, 1.0, 0.0)

    owner = owner_ref[...].reshape(1, 384)
    e = lax.broadcasted_iota(jnp.int32, (1, 384), 1)
    uniform = ((real(e) + 0.5) * (1.0 / 12.0)).astype(jnp.int32)
    chip, upper = owner // 2, uniform % 2
    d = (uniform // 2 - chip) & 15
    up = upper == 1
    plus = jnp.where(up, jnp.where(d <= 7, 1, 0), jnp.where((d >= 1) & (d <= 8), 1, 0)) == 1
    there = d + upper
    back = jnp.where(up, 16 - d, jnp.where(d == 0, 1, 17 - d))
    reach = jnp.where(plus, there, back)
    way = jnp.where(plus, 0, 1)
    stop = jnp.where(plus, chip, (16 - chip) & 15)
    train = way * 16 + stop
    key = (8 - reach) * 384 + e

    zero_row = jnp.zeros((1, 384), f32)
    direct = jnp.where(owner % 2 == way, 1.0, 0.0)
    rows = [real(owner), real(key), real(train), real(reach), real(e), direct, zero_row, zero_row]
    columns = jnp.transpose(jnp.concatenate(rows, axis=0))
    rank, slot, place = zero_row, zero_row, zero_row
    for c in range(0, 384, 32):
        part = columns[c : c + 32]
        same = part[:, 0:1] == rows[0]
        before = part[:, 1:2] < rows[1]
        rank = rank + jnp.sum(one(same & before), axis=0, keepdims=True)
        slot = slot + jnp.sum(one(same & (part[:, 4:5] < rows[4])), axis=0, keepdims=True)
        place = place + jnp.sum(one((part[:, 2:3] == rows[2]) & before), axis=0, keepdims=True)
    ranked = jnp.transpose(jnp.concatenate([rank, place] + [zero_row] * 6, axis=0))

    lane = lax.broadcasted_iota(jnp.int32, (1, 128), 1)
    quarter, link = lane // 32, lane % 32
    passing = [jnp.zeros((1, 128), f32) for _ in range(2)]
    ready = [[jnp.full((1, 128), 384.0, f32) for _ in range(7)] for _ in range(2)]
    for c in range(0, 384, 32):
        part, more = columns[c : c + 32], ranked[c : c + 32]
        held = part[:, 2:3] == real(link)
        for h in (0, 1):
            through = held & (part[:, 3:4] > real(quarter + 4 * h))
            passing[h] = passing[h] + jnp.sum(one(through), axis=0, keepdims=True)
        for kind in (0, 1):
            mine = jnp.where(held & (part[:, 5:6] == 1.0 - kind), more[:, 1:2], 384.0)
            for h in range(7):
                first = jnp.where(more[:, 0:1] >= real(quarter + 4 * h), mine, 384.0)
                ready[kind][h] = jnp.minimum(ready[kind][h], jnp.min(first, axis=0, keepdims=True))

    def split(vector):
        return [vector] + [pltpu.roll(vector, 128 - 32 * g, 1) for g in (1, 2, 3)]

    def moved(vector, hops):
        return jnp.where(lane % 16 >= hops, pltpu.roll(vector, hops, 1), pltpu.roll(vector, 112 + hops, 1))

    totals = split(passing[0]) + split(passing[1])
    total = jnp.sum(jnp.where(lane < 32, sum(totals), 0.0))
    place_of = {}
    for i in range(8):
        for v in range(i, 8):
            place_of[i, v] = len(place_of)
            row = moved(totals[v], i) if i else totals[v]
            count_ref[place_of[i, v] : place_of[i, v] + 1, :] = row
            if i == v and i:
                limit_ref[i - 1 : i, :] = row
    limit_ref[7:8, :] = totals[0]
    for kind in (0, 1):
        for h in range(7):
            for g, row in enumerate(split(ready[kind][h])):
                at = 32 * kind + 4 * h + g
                ready_ref[at : at + 1, :] = jnp.minimum(row, totals[0])

    edge = lax.broadcasted_iota(jnp.int32, (8, 128), 1) % 16 == 0
    zero = jnp.zeros((1, 128), f32)
    for t in range(LAG):
        recent_ref[t] = jnp.zeros((8, 128), f32)
    code_ref[STEPS:ROWS, :] = jnp.full((ROWS - STEPS, 128), -1.0, f32)
    limit = limit_ref[...]

    def group(g, sent):
        for s in range(LAG):
            old = recent_ref[s]
            came = jnp.where(edge, pltpu.roll(old, 113, 1), pltpu.roll(old, 1, 1))
            there_ref[s] = jnp.minimum(came, limit)
        for s in range(LAG):
            t = g * LAG + s
            direct = jnp.minimum(2 * (t // 5) + 1 + jnp.where(t % 5 >= 2, 1, 0), 24)
            via_twin = jnp.minimum(2 * (t // 5) + jnp.where(t % 5 >= 3, 1, 0), 24)
            scores = []
            for i in range(8):
                if i == 0:
                    most = jnp.minimum(ready_ref[pl.ds(direct, 1), :], ready_ref[pl.ds(32 + via_twin, 1), :])
                else:
                    most = there_ref[s, i - 1 : i, :]
                ahead = [
                    jnp.where(sent[i] < count_ref[place_of[i, v] : place_of[i, v] + 1, :], 8.0, 0.0)
                    for v in range(i, 8)
                ]
                scores.append(jnp.where(sent[i] < most, tree(jnp.add, ahead) + (7.0 - i), 0.0))
            best = jnp.maximum(tree(jnp.maximum, scores), 1.0)
            go = [jnp.where(score == best, 1.0, 0.0) for score in scores]
            code_ref[pl.ds(t, 1), :] = tree(jnp.add, [go[i] * (sent[i] + (64.0 * i + 1.0)) for i in range(8)]) - 1.0
            sent = [sent[i] + go[i] for i in range(8)]
            for i in range(8):
                recent_ref[s, i : i + 1, :] = sent[i]
        return tuple(sent)

    lax.fori_loop(0, STEPS // LAG, group, (zero,) * 8)

    code = code_ref[...]
    lanes = lax.broadcasted_iota(jnp.int32, (ROWS, 128), 1)
    slots = real(lax.broadcasted_iota(jnp.int32, (ROWS, 1), 0))
    used = (code >= 0.0) & (lanes < 32)
    sent_all = jnp.sum(one(used))
    needed = jnp.max(jnp.where(used, slots + 1.0, 0.0))
    needed = jnp.where(sent_all == total, needed, STEPS + 1.0)
    choice = sum(jnp.where(needed > size, 1.0, 0.0) for size in SIZES)
    core, home = me % 2, me // 2
    mirror = (16 - home) & 15
    at = jnp.where(core == 0, home, mirror)
    twin_at = jnp.where(core == 0, mirror, home)

    def column(index):
        return jnp.sum(jnp.where(lanes == index, code, 0.0), axis=1, keepdims=True)

    leaving = column(core * 16 + at)
    arriving = column(core * 16 + ((at + 15) & 15))
    other = column((1 - core) * 16 + ((twin_at + 15) & 15))
    hops = (jnp.where(plus, home, mirror) - stop) & 15
    mine = way == core
    local = jnp.where(owner % 2 == core, rank, 24.0 + rank)
    came = real(hops - 1) * 64.0 + place
    stored = jnp.sum(jnp.where(arriving == came, 2.0 * slots, 0.0), axis=0, keepdims=True)
    relayed = jnp.sum(jnp.where(other == came, 2.0 * slots, 0.0), axis=0, keepdims=True)
    where = jnp.where(hops == 0, local, jnp.where(mine, 48.0 + stored, 49.0 + relayed))
    goes = jnp.where(mine & (hops < reach), real(hops) * 64.0 + place, -2.0)
    index = jnp.sum(jnp.where(leaving == goes, where, 0.0), axis=1, keepdims=True)
    ranks = real(lax.broadcasted_iota(jnp.int32, (24, 1), 0))
    order = jnp.sum(jnp.where((owner == me) & (rank == ranks), slot, 0.0), axis=1, keepdims=True)
    wanted = lax.broadcasted_iota(jnp.int32, (40, 1), 0) + 12 * me - 12
    wanted = jnp.where(wanted < 0, wanted + 384, jnp.where(wanted >= 384, wanted - 384, wanted))
    location = jnp.sum(jnp.where(wanted == e, where, 0.0), axis=1, keepdims=True)
    first = jnp.concatenate([index, jnp.zeros((128 - ROWS, 1), f32)], axis=0)
    second = jnp.concatenate([order, location, jnp.full((8, 1), choice, f32), jnp.zeros((56, 1), f32)], axis=0)
    for r, part in enumerate((first, second)):
        whole = jnp.transpose(jnp.broadcast_to(part, (128, 128)))
        table_ref[r : r + 1, :] = whole[0:1].astype(jnp.int32)


def tables(owner, me_of):
    def area(*shape):
        return jax.ShapeDtypeStruct(shape, jnp.float32)

    def kernel(*refs):
        route_kernel(me_of, *refs)

    return pl.pallas_call(
        kernel,
        out_shape=(
            jax.ShapeDtypeStruct((2, 128), jnp.int32),
            area(ROWS, 128),
            area(8, 128),
            area(64, 128),
            area(40, 128),
            area(LAG, 8, 128),
            area(LAG, 8, 128),
        ),
        in_specs=[pl.BlockSpec(memory_space=pltpu.VMEM)],
        out_specs=(pl.BlockSpec(memory_space=pltpu.VMEM),) * 7,
    )(owner)[0]


def wide(real, imag):
    return jnp.concatenate([real, imag], axis=1)


def main_kernel(
    size,
    table,
    weights,
    offsets,
    ret_hbm,
    sig_hbm,
    coupling_ref,
    out_ref,
    ret,
    sig,
    outgoing,
    lower,
    upper,
    twin,
    landed,
    relayed,
    sending,
    pool,
    left_mats,
    right_mats,
    load_sem,
    low_send,
    up_send,
    low_recv,
    up_recv,
    twin_send,
    twin_recv,
    ring_send,
    ring_recv,
    relay_send,
    relay_recv,
):
    energy, slab = lax.axis_index("energy"), lax.axis_index("slab")
    core = lax.rem(energy, 2)
    step = 2 - 4 * core
    ahead = (lax.rem(energy + step + 32, 32), slab)
    behind = (lax.rem(energy - step + 32, 32), slab)
    partner = (energy + 1 - 2 * core, slab)
    slab_up = (energy, lax.rem(slab + 1, 16))
    slab_down = (energy, lax.rem(slab + 15, 16))
    has_lower = jnp.where(slab > 0, 0.5, 0.0)
    has_upper = jnp.where(slab < 15, 0.5, 0.0)

    load_sig = pltpu.make_async_copy(sig_hbm.at[0], sig, load_sem.at[0])
    load_ret = pltpu.make_async_copy(ret_hbm.at[0], ret, load_sem.at[1])
    load_sig.start()
    load_ret.start()

    barrier = pltpu.get_barrier_semaphore()
    for device in (ahead, behind, partner, slab_up, slab_down):
        pl.semaphore_signal(barrier, inc=1, device_id=device, device_id_type=MESH)

    def remote(source, target, send, receive, device):
        return pltpu.make_async_remote_copy(
            src_ref=source,
            dst_ref=target,
            send_sem=send,
            recv_sem=receive,
            device_id=device,
            device_id_type=MESH,
        )

    def to_upper(j):
        return remote(outgoing.at[j], lower.at[j], up_send.at[0], low_recv.at[j], slab_up)

    def to_lower(j):
        return remote(outgoing.at[j], upper.at[j], low_send.at[0], up_recv.at[j], slab_down)

    def to_twin(j):
        return remote(pool.at[j], twin.at[j], twin_send.at[0], twin_recv.at[j], partner)

    def to_ring(t):
        return remote(sending.at[t], landed.at[t], ring_send.at[lax.rem(t, FLIGHT)], ring_recv.at[t], ahead)

    def to_relay(t):
        return remote(landed.at[t], relayed.at[t], relay_send.at[lax.rem(t, FLIGHT)], relay_recv.at[t], partner)

    def spread(j):
        outgoing[j] = sig[table[1, j]]
        to_upper(j).start()
        to_lower(j).start()

    load_sig.wait()
    pl.semaphore_wait(barrier, 5)
    for j in range(AHEAD):
        spread(j)
    for k in range(4):
        m_real, m_imag = coupling_ref[k, 0], coupling_ref[k, 1]
        left_mats[k] = jnp.concatenate([wide(m_real, -m_imag), wide(m_imag, m_real)], axis=0)
        right_mats[:, 256 * k : 256 * k + 256] = jnp.concatenate(
            [wide(m_real, m_imag), wide(-m_imag, m_real)], axis=0
        )
    load_ret.wait()

    def form(j):
        to_upper(j).wait_recv()
        to_lower(j).wait_recv()
        beside = lower[j].astype(jnp.float32) * has_lower + upper[j].astype(jnp.float32) * has_upper
        total = (outgoing[j].astype(jnp.float32) + beside).astype(jnp.bfloat16)
        s_real, s_imag = total[0], total[1]
        block = ret[table[1, j]]
        r_real, r_imag = block[0], block[1]
        right = jnp.concatenate([wide(s_real, s_imag), wide(-s_imag, s_real)], axis=0)
        half = jnp.dot(wide(r_real, r_imag), right, preferred_element_type=jnp.float32).astype(jnp.bfloat16)
        back = jnp.concatenate([wide(r_real, r_imag), wide(-r_imag, r_real)], axis=0)
        full = lax.dot_general(half, back, (((1,), (1,)), ((), ())), preferred_element_type=jnp.float32)
        full = full.astype(jnp.bfloat16)
        pool[j, 0] = full[:, :128]
        pool[j, 1] = full[:, 128:]
        to_twin(j).start()

    def take_twin(j):
        to_twin(j).wait_recv()
        pool[24 + j] = twin[j]

    def take_ring(t):
        to_ring(t).wait_recv()
        to_relay(t).start()
        pool[48 + 2 * t] = landed[t]
        to_ring(t).wait_send()

    def take_relay(t):
        to_relay(t).wait_recv()
        pool[49 + 2 * t] = relayed[t]
        to_relay(t).wait_send()

    def send_ring(t):
        sending[t] = pool[table[0, t]]
        to_ring(t).start()

    def early(g, carry):
        def ring(k):
            t = 5 * g + k

            @pl.when(t >= LAG)
            def _():
                take_ring(t - LAG)

            send_ring(t)

            @pl.when(t >= LAG + PLAG)
            def _():
                take_relay(t - LAG - PLAG)

        @pl.when(g < (24 - AHEAD) // 2)
        def _():
            spread(2 * g + AHEAD)
            spread(2 * g + AHEAD + 1)

        form(2 * g)

        @pl.when(g >= 1)
        def _():
            take_twin(2 * g - 1)

        ring(0)
        ring(1)
        form(2 * g + 1)
        ring(2)
        take_twin(2 * g)
        ring(3)
        ring(4)
        return carry

    lax.fori_loop(0, 12, early, 0)
    take_twin(23)

    def late(t, carry):
        take_ring(t - LAG)
        send_ring(t)
        take_relay(t - LAG - PLAG)
        return carry

    lax.fori_loop(60, size, late, 0)

    remote(outgoing, lower, up_send.at[0], low_recv.at[0], slab_up).wait_send()
    remote(outgoing, upper, low_send.at[0], up_recv.at[0], slab_down).wait_send()
    remote(pool.at[pl.ds(0, 24)], twin, twin_send.at[0], twin_recv.at[0], partner).wait_send()

    def last(t, carry):
        take_ring(t)
        take_relay(t - PLAG)
        return carry

    lax.fori_loop(size - LAG, size, last, 0)

    def final(t, carry):
        take_relay(t)
        return carry

    lax.fori_loop(size - PLAG, size, final, 0)

    def weighted(i, k):
        offset = offsets[k]
        up = pool[table[1, 36 + i + offset]].astype(jnp.float32)
        down = pool[table[1, 36 + i - offset]].astype(jnp.float32)
        value = (weights[k] + 1.0) * up + weights[k] * down
        return value.astype(jnp.bfloat16).reshape(256, 128)

    def finish(p, carry):
        coupled = []
        for k in range(4):
            pair = wide(weighted(2 * p, k), weighted(2 * p + 1, k))
            left = jnp.dot(left_mats[k], pair, preferred_element_type=jnp.float32).astype(jnp.bfloat16)
            rows = [wide(left[:128, c : c + 128], left[128:, c : c + 128]) for c in (0, 128)]
            coupled.append(jnp.concatenate(rows, axis=0))
        whole = jnp.concatenate(coupled, axis=1)
        result = lax.dot_general(
            whole, right_mats[...], (((1,), (1,)), ((), ())), preferred_element_type=jnp.float32
        )
        for c in (0, 1):
            out_ref[0, 2 * p + c, 0] = result[128 * c : 128 * c + 128, :128]
            out_ref[0, 2 * p + c, 1] = result[128 * c : 128 * c + 128, 128:]
        return carry

    lax.fori_loop(0, 6, finish, 0, unroll=6)


def routed(size, identity, table, occupancy, offsets, retarded, self_lesser, coupling):
    def blocks(n):
        return pltpu.VMEM((n, 2, 128, 128), jnp.bfloat16)

    dma = pltpu.SemaphoreType.DMA
    return pl.pallas_call(
        functools.partial(main_kernel, size),
        out_shape=jax.ShapeDtypeStruct((1, 12, 2, 128, 128), jnp.float32),
        in_specs=[
            pl.BlockSpec(memory_space=pltpu.SMEM),
            pl.BlockSpec(memory_space=pltpu.SMEM),
            pl.BlockSpec(memory_space=pltpu.SMEM),
            pl.BlockSpec(memory_space=pl.ANY),
            pl.BlockSpec(memory_space=pl.ANY),
            pl.BlockSpec(memory_space=pltpu.VMEM),
        ],
        out_specs=pl.BlockSpec(memory_space=pltpu.VMEM),
        scratch_shapes=[
            blocks(24),
            blocks(24),
            blocks(24),
            blocks(24),
            blocks(24),
            blocks(24),
            blocks(size),
            blocks(size),
            blocks(size),
            blocks(48 + 2 * size),
            pltpu.VMEM((4, 256, 256), jnp.bfloat16),
            pltpu.VMEM((256, 1024), jnp.bfloat16),
            dma((2,)),
            dma((1,)),
            dma((1,)),
            dma((24,)),
            dma((24,)),
            dma((1,)),
            dma((24,)),
            dma((FLIGHT,)),
            dma((size,)),
            dma((FLIGHT,)),
            dma((size,)),
        ],
        compiler_params=pltpu.CompilerParams(
            collective_id=identity, has_side_effects=True, vmem_limit_bytes=60 * 1024 * 1024
        ),
    )(table, occupancy, offsets, retarded, self_lesser, coupling)


def body(retarded, self_lesser, coupling, occupancy, adaptive_owner, phonon_offsets):
    table = tables(adaptive_owner, lambda: lax.axis_index("energy"))
    choice = table[1, 64]

    def fast(size, identity):
        def call(_):
            return routed(size, identity, table, occupancy, phonon_offsets, retarded, self_lesser, coupling)

        return call

    def slow(_):
        return general(retarded, self_lesser, coupling, occupancy, adaptive_owner, phonon_offsets)

    branches = [fast(size, i) for i, size in enumerate(SIZES)] + [slow]
    return lax.switch(choice, branches, 0)


def solution(mesh):
    placed = (
        P("slab", "energy", None, None, None),
        P("slab", "energy", None, None, None),
        P(),
        P(),
        P(),
        P(),
    )
    return jax.shard_map(
        body,
        mesh=mesh,
        in_specs=placed,
        out_specs=P("slab", "energy", None, None, None),
        check_vma=False,
    )
```

```python
import functools

import jax
import jax.numpy as jnp
from jax import lax
from jax.experimental import pallas as pl
from jax.experimental.pallas import tpu as pltpu
from jax.sharding import PartitionSpec as P

MESH = pl.DeviceIdType.MESH
LAG = 5
FLIGHT = 10
PLAG = 3
AHEAD = 12
STEPS = 105
ROWS = 112
SIZES = (75, 80, 84, 104)


def with_halo(array, sides, width, wrap):
    for axis, dim in sides:
        peers, length = (lax.axis_size(axis), array.shape[dim])
        up = [(i, (i + 1) % peers) for i in range(peers if wrap else peers - 1)]
        down = [(j, i) for i, j in up]
        last = lax.slice_in_dim(array, length - width, length, axis=dim)
        initial = lax.slice_in_dim(array, 0, width, axis=dim)
        before = lax.ppermute(last, axis, up)
        after = lax.ppermute(initial, axis, down)
        array = jnp.concatenate([before, array, after], axis=dim)
    return array


def batched(left_block, right_block):
    return jnp.einsum("jab,jbc->jac", left_block, right_block, preferred_element_type=jnp.float32)


def batched_transposed(left_block, right_block):
    return jnp.einsum("jab,jcb->jac", left_block, right_block, preferred_element_type=jnp.float32)


def lesser_blocks(green_ret, sigma_total):
    ret_real, ret_imag = (green_ret[:, 0], green_ret[:, 1])
    sig_real, sig_imag = (sigma_total[:, 0], sigma_total[:, 1])
    half_real = batched(ret_real, sig_real) - batched(ret_imag, sig_imag)
    half_imag = batched(ret_real, sig_imag) + batched(ret_imag, sig_real)
    half_product = jnp.stack([half_real, half_imag], 1).astype(jnp.bfloat16)
    hp_real, hp_imag = (half_product[:, 0], half_product[:, 1])
    out_real = batched_transposed(hp_real, ret_real) + batched_transposed(hp_imag, ret_imag)
    out_imag = batched_transposed(hp_imag, ret_real) - batched_transposed(hp_real, ret_imag)
    return jnp.stack([out_real, out_imag], 1).astype(jnp.bfloat16)


def combined(stacked_rims):
    own_sigma = stacked_rims[1].astype(jnp.float32)
    beside = stacked_rims[0].astype(jnp.float32) + stacked_rims[2].astype(jnp.float32)
    return (own_sigma + 0.5 * beside).astype(jnp.bfloat16)


def sandwich(coupling_mode, weighted):
    m_real, m_imag = (coupling_mode[0], coupling_mode[1])
    w_real, w_imag = (weighted[:, 0], weighted[:, 1])
    left_real = jnp.einsum(
        "ab,jbc->jac", m_real, w_real, preferred_element_type=jnp.float32
    ) - jnp.einsum("ab,jbc->jac", m_imag, w_imag, preferred_element_type=jnp.float32)
    left_imag = jnp.einsum(
        "ab,jbc->jac", m_real, w_imag, preferred_element_type=jnp.float32
    ) + jnp.einsum("ab,jbc->jac", m_imag, w_real, preferred_element_type=jnp.float32)
    coupled = jnp.stack([left_real, left_imag], 1).astype(jnp.bfloat16)
    c_real, c_imag = (coupled[:, 0], coupled[:, 1])
    out_real = jnp.einsum(
        "jab,cb->jac", c_real, m_real, preferred_element_type=jnp.float32
    ) + jnp.einsum("jab,cb->jac", c_imag, m_imag, preferred_element_type=jnp.float32)
    out_imag = jnp.einsum(
        "jab,cb->jac", c_imag, m_real, preferred_element_type=jnp.float32
    ) - jnp.einsum("jab,cb->jac", c_real, m_imag, preferred_element_type=jnp.float32)
    return jnp.stack([out_real, out_imag], 1)


def general(retarded, self_lesser, coupling, occupancy, adaptive_owner, phonon_offsets):
    n_energy = lax.axis_size("energy")
    my_index = lax.axis_index("energy")
    energies = adaptive_owner.shape[0]
    per_device = energies // n_energy
    capacity = retarded.shape[1]
    slot_count = -(-capacity // n_energy)
    positions = jnp.arange(energies, dtype=jnp.int32)
    block_of = positions // per_device
    same_owner = adaptive_owner[:, None] == adaptive_owner[None, :]
    earlier = same_owner & (positions[None, :] < positions[:, None])
    slot_rank = jnp.sum(earlier.astype(jnp.int32), axis=1)
    same_block = block_of[None, :] == block_of[:, None]
    group_rank = jnp.sum((earlier & same_block).astype(jnp.int32), axis=1)
    target = block_of * slot_count + group_rank
    targets = jnp.arange(n_energy * slot_count, dtype=jnp.int32)
    matches = (adaptive_owner == my_index)[None, :] & (target[None, :] == targets[:, None])
    send_slot = jnp.sum(jnp.where(matches, slot_rank[None, :], 0), axis=1)
    first_energy = my_index * per_device
    own_owner = lax.dynamic_slice_in_dim(adaptive_owner, first_energy, per_device)
    own_rank = lax.dynamic_slice_in_dim(group_rank, first_energy, per_device)
    receive_slot = own_owner * slot_count + own_rank
    stacked_rims = with_halo(self_lesser, (("slab", 0),), 1, False)
    formed = lesser_blocks(retarded[0], combined(stacked_rims))
    outgoing = jnp.take(formed, send_slot, axis=0)
    arrived = lax.all_to_all(outgoing, "energy", split_axis=0, concat_axis=0, tiled=True)
    lesser = jnp.take(arrived, receive_slot, axis=0)
    widened = with_halo(lesser, (("energy", 0),), per_device, True)
    accumulated = jnp.zeros((per_device, 2, lesser.shape[2], lesser.shape[3]), jnp.float32)
    for phonon_mode in range(coupling.shape[0]):
        offset = phonon_offsets[phonon_mode]
        shifted_up = lax.dynamic_slice_in_dim(widened, per_device + offset, per_device, 0).astype(
            jnp.float32
        )
        shifted_down = lax.dynamic_slice_in_dim(widened, per_device - offset, per_device, 0).astype(
            jnp.float32
        )
        weight_one = occupancy[phonon_mode]
        weighted = ((weight_one + 1.0) * shifted_up + weight_one * shifted_down).astype(
            jnp.bfloat16
        )
        accumulated = accumulated + sandwich(coupling[phonon_mode], weighted)
    return accumulated[None]


def tree(combine, values):
    while len(values) > 1:
        pairs = [combine(a, b) for a, b in zip(values[::2], values[1::2])]
        values = pairs + ([values[-1]] if len(values) % 2 else [])
    return values[0]


def route_kernel(me_of, owner_ref, table_ref, code_ref, limit_ref, ready_ref, count_ref, recent_ref, there_ref):
    f32 = jnp.float32
    me = me_of()

    def real(value):
        return value.astype(f32)

    def one(mask):
        return jnp.where(mask, 1.0, 0.0)

    owner = owner_ref[...].reshape(1, 384)
    e = lax.broadcasted_iota(jnp.int32, (1, 384), 1)
    uniform = ((real(e) + 0.5) * (1.0 / 12.0)).astype(jnp.int32)
    chip, upper = owner // 2, uniform % 2
    d = (uniform // 2 - chip) & 15
    up = upper == 1
    plus = jnp.where(up, jnp.where(d <= 7, 1, 0), jnp.where((d >= 1) & (d <= 8), 1, 0)) == 1
    there = d + upper
    back = jnp.where(up, 16 - d, jnp.where(d == 0, 1, 17 - d))
    reach = jnp.where(plus, there, back)
    way = jnp.where(plus, 0, 1)
    stop = jnp.where(plus, chip, (16 - chip) & 15)
    train = way * 16 + stop
    key = (8 - reach) * 384 + e

    zero_row = jnp.zeros((1, 384), f32)
    direct = jnp.where(owner % 2 == way, 1.0, 0.0)
    rows = [real(owner), real(key), real(train), real(reach), real(e), direct, zero_row, zero_row]
    columns = jnp.transpose(jnp.concatenate(rows, axis=0))
    rank, slot, place = zero_row, zero_row, zero_row
    for c in range(0, 384, 32):
        part = columns[c : c + 32]
        same = part[:, 0:1] == rows[0]
        before = part[:, 1:2] < rows[1]
        rank = rank + jnp.sum(one(same & before), axis=0, keepdims=True)
        slot = slot + jnp.sum(one(same & (part[:, 4:5] < rows[4])), axis=0, keepdims=True)
        place = place + jnp.sum(one((part[:, 2:3] == rows[2]) & before), axis=0, keepdims=True)
    ranked = jnp.transpose(jnp.concatenate([rank, place] + [zero_row] * 6, axis=0))

    lane = lax.broadcasted_iota(jnp.int32, (1, 128), 1)
    quarter, link = lane // 32, lane % 32
    passing = [jnp.zeros((1, 128), f32) for _ in range(2)]
    ready = [[jnp.full((1, 128), 384.0, f32) for _ in range(7)] for _ in range(2)]
    for c in range(0, 384, 32):
        part, more = columns[c : c + 32], ranked[c : c + 32]
        held = part[:, 2:3] == real(link)
        for h in (0, 1):
            through = held & (part[:, 3:4] > real(quarter + 4 * h))
            passing[h] = passing[h] + jnp.sum(one(through), axis=0, keepdims=True)
        for kind in (0, 1):
            mine = jnp.where(held & (part[:, 5:6] == 1.0 - kind), more[:, 1:2], 384.0)
            for h in range(7):
                first = jnp.where(more[:, 0:1] >= real(quarter + 4 * h), mine, 384.0)
                ready[kind][h] = jnp.minimum(ready[kind][h], jnp.min(first, axis=0, keepdims=True))

    def split(vector):
        return [vector] + [pltpu.roll(vector, 128 - 32 * g, 1) for g in (1, 2, 3)]

    def moved(vector, hops):
        return jnp.where(lane % 16 >= hops, pltpu.roll(vector, hops, 1), pltpu.roll(vector, 112 + hops, 1))

    totals = split(passing[0]) + split(passing[1])
    total = jnp.sum(jnp.where(lane < 32, sum(totals), 0.0))
    place_of = {}
    for i in range(8):
        for v in range(i, 8):
            place_of[i, v] = len(place_of)
            row = moved(totals[v], i) if i else totals[v]
            count_ref[place_of[i, v] : place_of[i, v] + 1, :] = row
            if i == v and i:
                limit_ref[i - 1 : i, :] = row
    limit_ref[7:8, :] = totals[0]
    for kind in (0, 1):
        for h in range(7):
            for g, row in enumerate(split(ready[kind][h])):
                at = 32 * kind + 4 * h + g
                ready_ref[at : at + 1, :] = jnp.minimum(row, totals[0])

    edge = lax.broadcasted_iota(jnp.int32, (8, 128), 1) % 16 == 0
    zero = jnp.zeros((1, 128), f32)
    for t in range(LAG):
        recent_ref[t] = jnp.zeros((8, 128), f32)
    code_ref[STEPS:ROWS, :] = jnp.full((ROWS - STEPS, 128), -1.0, f32)
    limit = limit_ref[...]

    def group(g, sent):
        for s in range(LAG):
            old = recent_ref[s]
            came = jnp.where(edge, pltpu.roll(old, 113, 1), pltpu.roll(old, 1, 1))
            there_ref[s] = jnp.minimum(came, limit)
        for s in range(LAG):
            t = g * LAG + s
            direct = jnp.minimum(2 * (t // 5) + 1 + jnp.where(t % 5 >= 2, 1, 0), 24)
            via_twin = jnp.minimum(2 * (t // 5) + jnp.where(t % 5 >= 3, 1, 0), 24)
            scores = []
            for i in range(8):
                if i == 0:
                    most = jnp.minimum(ready_ref[pl.ds(direct, 1), :], ready_ref[pl.ds(32 + via_twin, 1), :])
                else:
                    most = there_ref[s, i - 1 : i, :]
                ahead = [
                    jnp.where(sent[i] < count_ref[place_of[i, v] : place_of[i, v] + 1, :], 8.0, 0.0)
                    for v in range(i, 8)
                ]
                scores.append(jnp.where(sent[i] < most, tree(jnp.add, ahead) + (7.0 - i), 0.0))
            best = jnp.maximum(tree(jnp.maximum, scores), 1.0)
            go = [jnp.where(score == best, 1.0, 0.0) for score in scores]
            code_ref[pl.ds(t, 1), :] = tree(jnp.add, [go[i] * (sent[i] + (64.0 * i + 1.0)) for i in range(8)]) - 1.0
            sent = [sent[i] + go[i] for i in range(8)]
            for i in range(8):
                recent_ref[s, i : i + 1, :] = sent[i]
        return tuple(sent)

    lax.fori_loop(0, STEPS // LAG, group, (zero,) * 8)

    code = code_ref[...]
    lanes = lax.broadcasted_iota(jnp.int32, (ROWS, 128), 1)
    slots = real(lax.broadcasted_iota(jnp.int32, (ROWS, 1), 0))
    used = (code >= 0.0) & (lanes < 32)
    sent_all = jnp.sum(one(used))
    needed = jnp.max(jnp.where(used, slots + 1.0, 0.0))
    needed = jnp.where(sent_all == total, needed, STEPS + 1.0)
    choice = sum(jnp.where(needed > size, 1.0, 0.0) for size in SIZES)
    core, home = me % 2, me // 2
    mirror = (16 - home) & 15
    at = jnp.where(core == 0, home, mirror)
    twin_at = jnp.where(core == 0, mirror, home)

    def column(index):
        return jnp.sum(jnp.where(lanes == index, code, 0.0), axis=1, keepdims=True)

    leaving = column(core * 16 + at)
    arriving = column(core * 16 + ((at + 15) & 15))
    other = column((1 - core) * 16 + ((twin_at + 15) & 15))
    hops = (jnp.where(plus, home, mirror) - stop) & 15
    mine = way == core
    local = jnp.where(owner % 2 == core, rank, 24.0 + rank)
    came = real(hops - 1) * 64.0 + place
    stored = jnp.sum(jnp.where(arriving == came, 2.0 * slots, 0.0), axis=0, keepdims=True)
    relayed = jnp.sum(jnp.where(other == came, 2.0 * slots, 0.0), axis=0, keepdims=True)
    where = jnp.where(hops == 0, local, jnp.where(mine, 48.0 + stored, 49.0 + relayed))
    goes = jnp.where(mine & (hops < reach), real(hops) * 64.0 + place, -2.0)
    index = jnp.sum(jnp.where(leaving == goes, where, 0.0), axis=1, keepdims=True)
    ranks = real(lax.broadcasted_iota(jnp.int32, (24, 1), 0))
    order = jnp.sum(jnp.where((owner == me) & (rank == ranks), slot, 0.0), axis=1, keepdims=True)
    wanted = lax.broadcasted_iota(jnp.int32, (40, 1), 0) + 12 * me - 12
    wanted = jnp.where(wanted < 0, wanted + 384, jnp.where(wanted >= 384, wanted - 384, wanted))
    location = jnp.sum(jnp.where(wanted == e, where, 0.0), axis=1, keepdims=True)
    first = jnp.concatenate([index, jnp.zeros((128 - ROWS, 1), f32)], axis=0)
    second = jnp.concatenate([order, location, jnp.full((8, 1), choice, f32), jnp.zeros((56, 1), f32)], axis=0)
    for r, part in enumerate((first, second)):
        whole = jnp.transpose(jnp.broadcast_to(part, (128, 128)))
        table_ref[r : r + 1, :] = whole[0:1].astype(jnp.int32)


def tables(owner, me_of):
    def area(*shape):
        return jax.ShapeDtypeStruct(shape, jnp.float32)

    def kernel(*refs):
        route_kernel(me_of, *refs)

    return pl.pallas_call(
        kernel,
        out_shape=(
            jax.ShapeDtypeStruct((2, 128), jnp.int32),
            area(ROWS, 128),
            area(8, 128),
            area(64, 128),
            area(40, 128),
            area(LAG, 8, 128),
            area(LAG, 8, 128),
        ),
        in_specs=[pl.BlockSpec(memory_space=pltpu.VMEM)],
        out_specs=(pl.BlockSpec(memory_space=pltpu.VMEM),) * 7,
    )(owner)[0]


def wide(real, imag):
    return jnp.concatenate([real, imag], axis=1)


def main_kernel(
    size,
    table,
    weights,
    offsets,
    ret_hbm,
    sig_hbm,
    coupling_ref,
    out_ref,
    ret,
    sig,
    outgoing,
    lower,
    upper,
    twin,
    landed,
    relayed,
    sending,
    pool,
    left_mats,
    right_mats,
    load_sem,
    low_send,
    up_send,
    low_recv,
    up_recv,
    twin_send,
    twin_recv,
    ring_send,
    ring_recv,
    relay_send,
    relay_recv,
):
    energy, slab = lax.axis_index("energy"), lax.axis_index("slab")
    core = lax.rem(energy, 2)
    step = 2 - 4 * core
    ahead = (lax.rem(energy + step + 32, 32), slab)
    behind = (lax.rem(energy - step + 32, 32), slab)
    partner = (energy + 1 - 2 * core, slab)
    slab_up = (energy, lax.rem(slab + 1, 16))
    slab_down = (energy, lax.rem(slab + 15, 16))
    has_lower = jnp.where(slab > 0, 0.5, 0.0)
    has_upper = jnp.where(slab < 15, 0.5, 0.0)

    load_sig = pltpu.make_async_copy(sig_hbm.at[0], sig, load_sem.at[0])
    load_ret = pltpu.make_async_copy(ret_hbm.at[0], ret, load_sem.at[1])
    load_sig.start()
    load_ret.start()

    barrier = pltpu.get_barrier_semaphore()
    for device in (ahead, behind, partner, slab_up, slab_down):
        pl.semaphore_signal(barrier, inc=1, device_id=device, device_id_type=MESH)

    def remote(source, target, send, receive, device):
        return pltpu.make_async_remote_copy(
            src_ref=source,
            dst_ref=target,
            send_sem=send,
            recv_sem=receive,
            device_id=device,
            device_id_type=MESH,
        )

    def to_upper(j):
        return remote(outgoing.at[j], lower.at[j], up_send.at[0], low_recv.at[j], slab_up)

    def to_lower(j):
        return remote(outgoing.at[j], upper.at[j], low_send.at[0], up_recv.at[j], slab_down)

    def to_twin(j):
        return remote(pool.at[j], twin.at[j], twin_send.at[0], twin_recv.at[j], partner)

    def to_ring(t):
        return remote(sending.at[t], landed.at[t], ring_send.at[lax.rem(t, FLIGHT)], ring_recv.at[t], ahead)

    def to_relay(t):
        return remote(landed.at[t], relayed.at[t], relay_send.at[lax.rem(t, FLIGHT)], relay_recv.at[t], partner)

    def spread(j):
        outgoing[j] = sig[table[1, j]]
        to_upper(j).start()
        to_lower(j).start()

    load_sig.wait()
    pl.semaphore_wait(barrier, 5)
    for j in range(AHEAD):
        spread(j)
    for k in range(4):
        m_real, m_imag = coupling_ref[k, 0], coupling_ref[k, 1]
        left_mats[k] = jnp.concatenate([wide(m_real, -m_imag), wide(m_imag, m_real)], axis=0)
        right_mats[:, 256 * k : 256 * k + 256] = jnp.concatenate(
            [wide(m_real, m_imag), wide(-m_imag, m_real)], axis=0
        )
    load_ret.wait()

    def form(j):
        to_upper(j).wait_recv()
        to_lower(j).wait_recv()
        beside = lower[j].astype(jnp.float32) * has_lower + upper[j].astype(jnp.float32) * has_upper
        total = (outgoing[j].astype(jnp.float32) + beside).astype(jnp.bfloat16)
        s_real, s_imag = total[0], total[1]
        block = ret[table[1, j]]
        r_real, r_imag = block[0], block[1]
        right = jnp.concatenate([wide(s_real, s_imag), wide(-s_imag, s_real)], axis=0)
        half = jnp.dot(wide(r_real, r_imag), right, preferred_element_type=jnp.float32).astype(jnp.bfloat16)
        back = jnp.concatenate([wide(r_real, r_imag), wide(-r_imag, r_real)], axis=0)
        full = lax.dot_general(half, back, (((1,), (1,)), ((), ())), preferred_element_type=jnp.float32)
        full = full.astype(jnp.bfloat16)
        pool[j, 0] = full[:, :128]
        pool[j, 1] = full[:, 128:]
        to_twin(j).start()

    def take_twin(j):
        to_twin(j).wait_recv()
        pool[24 + j] = twin[j]

    def take_ring(t):
        to_ring(t).wait_recv()
        to_relay(t).start()
        pool[48 + 2 * t] = landed[t]
        to_ring(t).wait_send()

    def take_relay(t):
        to_relay(t).wait_recv()
        pool[49 + 2 * t] = relayed[t]
        to_relay(t).wait_send()

    def send_ring(t):
        sending[t] = pool[table[0, t]]
        to_ring(t).start()

    def early(g, carry):
        def ring(k):
            t = 5 * g + k

            @pl.when(t >= LAG)
            def _():
                take_ring(t - LAG)

            send_ring(t)

            @pl.when(t >= LAG + PLAG)
            def _():
                take_relay(t - LAG - PLAG)

        @pl.when(g < (24 - AHEAD) // 2)
        def _():
            spread(2 * g + AHEAD)
            spread(2 * g + AHEAD + 1)

        form(2 * g)

        @pl.when(g >= 1)
        def _():
            take_twin(2 * g - 1)

        ring(0)
        ring(1)
        form(2 * g + 1)
        ring(2)
        take_twin(2 * g)
        ring(3)
        ring(4)
        return carry

    lax.fori_loop(0, 12, early, 0)
    take_twin(23)

    def late(t, carry):
        take_ring(t - LAG)
        send_ring(t)
        take_relay(t - LAG - PLAG)
        return carry

    lax.fori_loop(60, size, late, 0)

    remote(outgoing, lower, up_send.at[0], low_recv.at[0], slab_up).wait_send()
    remote(outgoing, upper, low_send.at[0], up_recv.at[0], slab_down).wait_send()
    remote(pool.at[pl.ds(0, 24)], twin, twin_send.at[0], twin_recv.at[0], partner).wait_send()

    def last(t, carry):
        take_ring(t)
        take_relay(t - PLAG)
        return carry

    lax.fori_loop(size - LAG, size, last, 0)

    def final(t, carry):
        take_relay(t)
        return carry

    lax.fori_loop(size - PLAG, size, final, 0)

    def weighted(i, k):
        offset = offsets[k]
        up = pool[table[1, 36 + i + offset]].astype(jnp.float32)
        down = pool[table[1, 36 + i - offset]].astype(jnp.float32)
        value = (weights[k] + 1.0) * up + weights[k] * down
        return value.astype(jnp.bfloat16).reshape(256, 128)

    def finish(p, carry):
        coupled = []
        for k in range(4):
            pair = wide(weighted(2 * p, k), weighted(2 * p + 1, k))
            left = jnp.dot(left_mats[k], pair, preferred_element_type=jnp.float32).astype(jnp.bfloat16)
            rows = [wide(left[:128, c : c + 128], left[128:, c : c + 128]) for c in (0, 128)]
            coupled.append(jnp.concatenate(rows, axis=0))
        whole = jnp.concatenate(coupled, axis=1)
        result = lax.dot_general(
            whole, right_mats[...], (((1,), (1,)), ((), ())), preferred_element_type=jnp.float32
        )
        for c in (0, 1):
            out_ref[0, 2 * p + c, 0] = result[128 * c : 128 * c + 128, :128]
            out_ref[0, 2 * p + c, 1] = result[128 * c : 128 * c + 128, 128:]
        return carry

    lax.fori_loop(0, 6, finish, 0, unroll=6)


def routed(size, identity, table, occupancy, offsets, retarded, self_lesser, coupling):
    def blocks(n):
        return pltpu.VMEM((n, 2, 128, 128), jnp.bfloat16)

    dma = pltpu.SemaphoreType.DMA
    return pl.pallas_call(
        functools.partial(main_kernel, size),
        out_shape=jax.ShapeDtypeStruct((1, 12, 2, 128, 128), jnp.float32),
        in_specs=[
            pl.BlockSpec(memory_space=pltpu.SMEM),
            pl.BlockSpec(memory_space=pltpu.SMEM),
            pl.BlockSpec(memory_space=pltpu.SMEM),
            pl.BlockSpec(memory_space=pl.ANY),
            pl.BlockSpec(memory_space=pl.ANY),
            pl.BlockSpec(memory_space=pltpu.VMEM),
        ],
        out_specs=pl.BlockSpec(memory_space=pltpu.VMEM),
        scratch_shapes=[
            blocks(24),
            blocks(24),
            blocks(24),
            blocks(24),
            blocks(24),
            blocks(24),
            blocks(size),
            blocks(size),
            blocks(size),
            blocks(48 + 2 * size),
            pltpu.VMEM((4, 256, 256), jnp.bfloat16),
            pltpu.VMEM((256, 1024), jnp.bfloat16),
            dma((2,)),
            dma((1,)),
            dma((1,)),
            dma((24,)),
            dma((24,)),
            dma((1,)),
            dma((24,)),
            dma((FLIGHT,)),
            dma((size,)),
            dma((FLIGHT,)),
            dma((size,)),
        ],
        compiler_params=pltpu.CompilerParams(
            collective_id=identity, has_side_effects=True, vmem_limit_bytes=60 * 1024 * 1024
        ),
    )(table, occupancy, offsets, retarded, self_lesser, coupling)


def body(retarded, self_lesser, coupling, occupancy, adaptive_owner, phonon_offsets):
    table = tables(adaptive_owner, lambda: lax.axis_index("energy"))
    choice = table[1, 64]

    def fast(size, identity):
        def call(_):
            return routed(size, identity, table, occupancy, phonon_offsets, retarded, self_lesser, coupling)

        return call

    def slow(_):
        return general(retarded, self_lesser, coupling, occupancy, adaptive_owner, phonon_offsets)

    branches = [fast(size, i) for i, size in enumerate(SIZES)] + [slow]
    return lax.switch(choice, branches, 0)


def solution(mesh):
    placed = (
        P("slab", "energy", None, None, None),
        P("slab", "energy", None, None, None),
        P(),
        P(),
        P(),
        P(),
    )
    return jax.shard_map(
        body,
        mesh=mesh,
        in_specs=placed,
        out_specs=P("slab", "energy", None, None, None),
        check_vma=False,
    )
```
